512 devices in a mesh: region: 32 (over x, y), band: 16 (over z, core).
Axes of the slice: x: 4, y: 8, z: 8, core: 2. Of those that a mesh axis runs over, the one named last changes fastest.
Arguments:
- vertex_inputs: bfloat16 [131072, 512], P(('region', 'band')), may hold values from -20 to 20
- partition_embed_matrix: bfloat16 [512, 512], replicated, may hold values from -0.25 to 0.25
- selector_embed_matrix: bfloat16 [512, 512], replicated, may hold values from -0.25 to 0.25
- partition_affinity_matrix: bfloat16 [64, 64], replicated, may hold values from -0.75 to 0.75
- sharpness_divisor: float32 [8], replicated, may hold values from 0.5 to 2
- latent_query_key_value_maps: float32 [3, 64, 64], replicated, may hold values from -0.75 to 0.75
- result_cotangent: bfloat16 [131072, 512], P(('region', 'band')), may hold values from -6 to 6
Outputs:
- grad_points: bfloat16 [131072, 512], P(('region', 'band'))
- grad_proj: float32 [512, 1024], P('region')
- grad_w_slice: float32 [64, 64], replicated
- grad_w_token: float32 [3, 64, 64], replicated
The draws below stay inside these ranges and needn't reach their ends.
All inputs are finite; a program needn't handle non-finite values.
Results may differ from the reference program's by a relative error of at most 0.013.
The reference program's roundings to bfloat16 on the way count: a program that leaves them out, or rounds other values in their place, can miss the bound.
Values sent between devices are 32-bit elements; how exact they have to be, the bound alone decides.
A program may use at most 64 MiB of HBM per device.

```python
import math
import jax
import jax.numpy as jnp
from jax import lax

D = 512
ATTN_GROUP_COUNT = 8
C = 64
G = 64
HC = 512
POINTS = 131072


def draw_vertex_inputs(key, part):
    first_key, second_key, third_key, fourth_key = jax.random.split(key, 4)
    row_scale = jnp.exp(jax.random.uniform(second_key, (POINTS, 1), jnp.float32, math.log(0.3), math.log(4.0)))
    column_mean = jax.random.normal(third_key, (1, D), jnp.float32)
    column_scale = jnp.exp(jax.random.uniform(fourth_key, (1, D), jnp.float32, math.log(0.3), math.log(3.0)))
    base_values = jax.random.normal(first_key, (POINTS, D), jnp.float32)
    mixed_values = (base_values + 0.7 * jnp.roll(base_values, 1, axis=1)) * column_scale + 0.4 * column_mean
    return jnp.clip(mixed_values * row_scale, -20.0, 20.0).astype(jnp.bfloat16)


def block_levels(key, dims, cuts, low, largest):
    def one(dim, shards_of):
        draws = jax.random.uniform(jax.random.fold_in(jax.random.fold_in(key, 6), dim), (shards_of,), jnp.float32, low / len(cuts), largest / len(cuts))
        return jnp.repeat(jnp.exp(draws), dims[dim] // shards_of).reshape((-1,) + (1,) * (len(dims) - dim - 1))

    level = one(*cuts[0])
    for cut in cuts[1:]:
        level = level * one(*cut)
    return level


def normal_values(own_key, dims, deviation, most, cuts=(), kind=jnp.bfloat16):
    result = jax.random.normal(own_key, dims, jnp.float32) * deviation
    if len(cuts) > 0:
        result = block_levels(own_key, dims, cuts, -0.22, 0.18) * result
    return jnp.clip(result, min=-most, max=most).astype(kind)


def setup_inputs(seed: int = 0) -> dict:
    key_list = jax.random.split(jax.random.key(seed), 8)
    return {
        "vertex_inputs": draw_vertex_inputs(jax.random.fold_in(key_list[7], 71), 0),
        "partition_embed_matrix": normal_values(key_list[1], (D, HC), D ** -0.5, 0.25),
        "selector_embed_matrix": normal_values(key_list[2], (D, HC), D ** -0.5, 0.25),
        "partition_affinity_matrix": normal_values(key_list[3], (C, G), C ** -0.5, 0.75),
        "sharpness_divisor": jnp.clip(jnp.exp(jax.random.uniform(key_list[4], (ATTN_GROUP_COUNT,), jnp.float32, math.log(0.5), math.log(2.0))), 0.5, 2.0),
        "latent_query_key_value_maps": normal_values(key_list[5], (3, C, C), C ** -0.5, 0.75, (), jnp.float32),
        "result_cotangent": normal_values(key_list[6], (POINTS, HC), 1.0, 6.0, ((0, 512),)),
    }


partition_affinity_bound = 8.0
score_cap = 10.0
epsilon = 1e-05

def to_bfloat(values):
    return lax.optimization_barrier(values.astype(jnp.bfloat16))

def token_mix(tokens, latent_query_key_value_maps):
    highest = lax.Precision.HIGHEST
    queries = jnp.einsum('hgc,cd->hgd', tokens, latent_query_key_value_maps[0], precision=highest)
    key_rows = jnp.einsum('hgc,cd->hgd', tokens, latent_query_key_value_maps[1], precision=highest)
    values = jnp.einsum('hgc,cd->hgd', tokens, latent_query_key_value_maps[2], precision=highest)
    scores = jnp.einsum('hgd,hkd->hgk', queries, key_rows, precision=highest) / math.sqrt(C)
    capped = score_cap * jnp.tanh(scores / score_cap)
    exp_scores = jnp.exp(capped)
    attention = exp_scores / lax.optimization_barrier(jnp.sum(exp_scores, axis=-1, keepdims=True))
    mixing = jnp.einsum('hgk,hkd->hgd', attention, values, precision=highest)
    return tokens + mixing

def reference(vertex_inputs, partition_embed_matrix, selector_embed_matrix, partition_affinity_matrix, sharpness_divisor, latent_query_key_value_maps, result_cotangent):
    feature = jnp.dot(vertex_inputs, partition_embed_matrix, preferred_element_type=jnp.float32).astype(jnp.bfloat16)
    middle = jnp.dot(vertex_inputs, selector_embed_matrix, preferred_element_type=jnp.float32).astype(jnp.bfloat16)
    middle_heads = middle.reshape(POINTS, ATTN_GROUP_COUNT, C).astype(jnp.float32)
    feature_heads = feature.reshape(POINTS, ATTN_GROUP_COUNT, C).astype(jnp.float32)
    grad_heads = result_cotangent.reshape(POINTS, ATTN_GROUP_COUNT, C).astype(jnp.float32)
    slice_table = partition_affinity_matrix.astype(jnp.float32)
    unclamped_attention_affinity = jnp.einsum('nhc,cg->nhg', middle_heads, slice_table)
    smooth_clamping_function = jnp.tanh(unclamped_attention_affinity / (partition_affinity_bound * sharpness_divisor[None, :, None]))
    exp_logit = jnp.exp(partition_affinity_bound * smooth_clamping_function)
    weight = exp_logit / lax.optimization_barrier(jnp.sum(exp_logit, axis=-1, keepdims=True))
    weight_wide = to_bfloat(weight).astype(jnp.float32)
    slice_mass = lax.optimization_barrier(jnp.sum(weight, axis=0))
    token_sum = jnp.einsum('nhg,nhc->hgc', weight_wide, feature_heads)
    back_sum = jnp.einsum('nhg,nhc->hgc', weight_wide, grad_heads)
    denominator = slice_mass + epsilon
    tokens = token_sum / denominator[:, :, None]
    out_token, pullback = jax.vjp(token_mix, tokens, latent_query_key_value_maps)
    grad_token, grad_w_token = pullback(back_sum)
    out_wide = to_bfloat(out_token).astype(jnp.float32)
    grad_sum_wide = to_bfloat(grad_token / denominator[:, :, None]).astype(jnp.float32)
    grad_mass = -lax.optimization_barrier(jnp.sum(grad_token * tokens, axis=-1)) / denominator
    grad_weight = jnp.einsum('nhc,hgc->nhg', grad_heads, out_wide)
    grad_weight = grad_weight + jnp.einsum('nhc,hgc->nhg', feature_heads, grad_sum_wide)
    grad_weight = grad_weight + grad_mass[None]
    preactivation_cotangent = weight * (grad_weight - lax.optimization_barrier(jnp.sum(weight * grad_weight, axis=-1, keepdims=True)))
    unprocessed_cotangent = (preactivation_cotangent * (1.0 - smooth_clamping_function * smooth_clamping_function) / sharpness_divisor[None, :, None]).astype(jnp.bfloat16)
    grad_raw_wide = unprocessed_cotangent.astype(jnp.float32)
    grad_feature = jnp.einsum('nhg,hgc->nhc', weight_wide, grad_sum_wide).reshape(POINTS, HC).astype(jnp.bfloat16)
    grad_mid = jnp.einsum('nhg,cg->nhc', grad_raw_wide, slice_table).reshape(POINTS, HC).astype(jnp.bfloat16)
    grad_points = jnp.dot(grad_feature, partition_embed_matrix.T, preferred_element_type=jnp.float32)
    grad_points = (grad_points + jnp.dot(grad_mid, selector_embed_matrix.T, preferred_element_type=jnp.float32)).astype(jnp.bfloat16)
    grad_proj = jnp.concatenate([jnp.dot(vertex_inputs.T, grad_feature, preferred_element_type=jnp.float32), jnp.dot(vertex_inputs.T, grad_mid, preferred_element_type=jnp.float32)], axis=1)
    grad_w_slice = jnp.einsum('nhc,nhg->cg', middle_heads, grad_raw_wide)
    return (grad_points, grad_proj, grad_w_slice, grad_w_token)
```

```python
import math

import jax
import jax.numpy as jnp
from jax import lax
from jax.experimental import pallas as pl
from jax.experimental.pallas import tpu as pltpu
from jax.sharding import PartitionSpec as P

partition_affinity_bound = 8.0
score_cap = 10.0
epsilon = 1e-05

NX, NY, NZ = 4, 8, 8
MESH = pl.DeviceIdType.MESH


def token_mix(tokens, latent_query_key_value_maps):
    highest = lax.Precision.HIGHEST
    head_width = tokens.shape[2]
    queries = jnp.einsum("hgc,cd->hgd", tokens, latent_query_key_value_maps[0], precision=highest)
    key_rows = jnp.einsum("hgc,cd->hgd", tokens, latent_query_key_value_maps[1], precision=highest)
    values = jnp.einsum("hgc,cd->hgd", tokens, latent_query_key_value_maps[2], precision=highest)
    scores = jnp.einsum("hgd,hkd->hgk", queries, key_rows, precision=highest) / math.sqrt(
        head_width
    )
    capped = score_cap * jnp.tanh(scores / score_cap)
    exp_scores = jnp.exp(capped)
    attention = exp_scores / jnp.sum(exp_scores, axis=-1, keepdims=True)
    mixing = jnp.einsum("hgk,hkd->hgd", attention, values, precision=highest)
    return tokens + mixing


class Place:
    def __init__(self):
        region, band = lax.axis_index("region"), lax.axis_index("band")
        self.x, self.y = lax.div(region, NY), lax.rem(region, NY)
        self.z, self.c = lax.div(band, 2), lax.rem(band, 2)

    def device(self, x=None, y=None, z=None, c=None):
        x = self.x if x is None else x
        y = self.y if y is None else y
        z = self.z if z is None else z
        c = self.c if c is None else c
        return {"region": x * NY + y, "band": z * 2 + c}

    def along(self, axis):
        size = {"x": NX, "y": NY, "z": NZ}[axis]
        here = getattr(self, axis)
        order = sorted(range(1, size), key=lambda k: -min(k, size - k))
        for k in order:
            there = lax.rem(here + k, size)
            yield k, there, self.device(**{axis: there})

    def greet(self):
        barrier = pltpu.get_barrier_semaphore()
        count = 0
        partners = [self.device(c=1 - self.c)]
        for axis in "xyz":
            partners += [d for _, _, d in self.along(axis)]
        for d in partners:
            pl.semaphore_signal(barrier, inc=1, device_id=d, device_id_type=MESH)
            count += 1
        pl.semaphore_wait(barrier, count)


class Sends:
    def __init__(self, send_sem, recv_sem):
        self.send_sem, self.recv_sem, self.used, self.open = send_sem, recv_sem, 0, []

    def start(self, src, dst, device):
        i = self.used
        self.used += 1
        copy = pltpu.make_async_remote_copy(
            src_ref=src,
            dst_ref=dst,
            send_sem=self.send_sem.at[i],
            recv_sem=self.recv_sem.at[i],
            device_id=device,
            device_id_type=MESH,
        )
        copy.start()
        self.open.append(copy)
        return copy

    def recv(self, copies):
        for copy in copies:
            copy.wait_recv()

    def finish(self):
        for copy in self.open:
            copy.wait_send()


def total_kernel(part, mass, full_out, mass_out, rc, rcm, s1, m1, rz, rzm, s2, m2, rx, rxm, s3, ry, full, send_sem, recv_sem):
    at = Place()
    at.greet()
    sends = Sends(send_sem, recv_sem)
    other = 1 - at.c
    partner = at.device(c=other)
    sends.recv([
        sends.start(part.at[other], rc, partner),
        sends.start(mass, rcm, partner),
    ])
    s1[...] = part[at.c] + rc[...]
    m1[...] = mass[...] + rcm[...]

    copies = []
    for k, there, device in at.along("z"):
        copies.append(sends.start(s1.at[there], rz.at[k - 1], device))
        copies.append(sends.start(m1, rzm.at[at.z], device))
    rzm[at.z] = m1[...]
    sends.recv(copies)
    s2[...] = s1[at.z] + jnp.sum(rz[...], axis=0)
    m2[...] = jnp.sum(rzm[...], axis=0)

    copies = []
    for k, there, device in at.along("x"):
        copies.append(sends.start(s2.at[there], rx.at[k - 1], device))
        copies.append(sends.start(m2, rxm.at[at.x], device))
    rxm[at.x] = m2[...]
    sends.recv(copies)
    s3[0] = s2[at.x] + jnp.sum(rx[...], axis=0)
    s3[1] = jnp.sum(rxm[...], axis=0)

    copies = []
    for k, there, device in at.along("y"):
        copies.append(sends.start(s3, ry.at[at.y], device))
    ry[at.y] = s3[...]
    sends.recv(copies)
    done = jnp.sum(ry[...], axis=0)
    mass_out[...] = done[1]

    full[at.c, at.z, at.x] = done[0]
    mine = full.at[at.c, at.z, at.x]
    sends.recv([sends.start(mine, mine, d) for _, _, d in at.along("x")])
    mine = full.at[at.c, at.z]
    sends.recv([sends.start(mine, mine, d) for _, _, d in at.along("z")])
    mine = full.at[at.c]
    sends.recv([sends.start(mine, mine, partner)])
    full_out[...] = full[...]
    sends.finish()


def total(part, mass):
    tile = (8, 128)
    f32 = jnp.float32
    copies = 2 + 2 * 7 + 2 * 3 + 7 + 3 + 7 + 1
    vmem = pl.BlockSpec(memory_space=pltpu.VMEM)
    return pl.pallas_call(
        total_kernel,
        out_shape=(
            jax.ShapeDtypeStruct((2, NZ, NX) + tile, f32),
            jax.ShapeDtypeStruct(tile, f32),
        ),
        in_specs=[vmem, vmem],
        out_specs=(vmem, vmem),
        scratch_shapes=[
            pltpu.VMEM((NZ, NX) + tile, f32),
            pltpu.VMEM(tile, f32),
            pltpu.VMEM((NZ, NX) + tile, f32),
            pltpu.VMEM(tile, f32),
            pltpu.VMEM((NZ - 1, NX) + tile, f32),
            pltpu.VMEM((NZ,) + tile, f32),
            pltpu.VMEM((NX,) + tile, f32),
            pltpu.VMEM(tile, f32),
            pltpu.VMEM((NX - 1,) + tile, f32),
            pltpu.VMEM((NX,) + tile, f32),
            pltpu.VMEM((2,) + tile, f32),
            pltpu.VMEM((NY, 2) + tile, f32),
            pltpu.VMEM((2, NZ, NX) + tile, f32),
            pltpu.SemaphoreType.DMA((copies,)),
            pltpu.SemaphoreType.DMA((copies,)),
        ],
        compiler_params=pltpu.CompilerParams(collective_id=1, has_side_effects=True),
        name="total",
    )(part, mass)


def scatter_kernel(proj, table, proj_out, table_out, rc, rcw, s1, w1, rz, ry, rwz, a2, b2, w2, ry2, rz2, rwy, ab, w3, rx, rwx, g, send_sem, recv_sem):
    at = Place()
    at.greet()
    sends = Sends(send_sem, recv_sem)
    other = 1 - at.c
    partner = at.device(c=other)
    sends.recv([
        sends.start(proj.at[:, :, other], rc, partner),
        sends.start(table, rcw, partner),
    ])
    for x in range(NX):
        for z in range(NZ):
            columns = slice(z * 128, (z + 1) * 128)
            s1[x, :, z] = proj[x, :, at.c, :, columns] + rc[x, :, :, columns]
    w1[...] = table[...] + rcw[...]

    copies = []
    half = NX // 2
    for (k, zt, zd), (_, yt, yd) in zip(at.along("z"), at.along("y")):
        copies.append(sends.start(s1.at[pl.ds(0, half), :, zt], rz.at[k - 1], zd))
        copies.append(sends.start(s1.at[pl.ds(half, half), yt], ry.at[k - 1], yd))
        copies.append(sends.start(w1.at[zt], rwz.at[k - 1], zd))
    sends.recv(copies)
    a2[...] = s1[pl.ds(0, half), :, at.z] + jnp.sum(rz[...], axis=0)
    b2[...] = s1[pl.ds(half, half), at.y] + jnp.sum(ry[...], axis=0)
    w2[...] = w1[at.z] + jnp.sum(rwz[...], axis=0)

    copies = []
    for (k, zt, zd), (_, yt, yd) in zip(at.along("z"), at.along("y")):
        copies.append(sends.start(a2.at[:, yt], ry2.at[k - 1], yd))
        copies.append(sends.start(b2.at[:, zt], rz2.at[k - 1], zd))
        copies.append(sends.start(w2, rwy.at[at.y], yd))
    rwy[at.y] = w2[...]
    sends.recv(copies)
    ab[pl.ds(0, half)] = a2[:, at.y] + jnp.sum(ry2[...], axis=0)
    ab[pl.ds(half, half)] = b2[:, at.z] + jnp.sum(rz2[...], axis=0)
    w3[...] = jnp.sum(rwy[...], axis=0)

    copies = []
    for k, there, device in at.along("x"):
        copies.append(sends.start(ab.at[there], rx.at[k - 1], device))
        copies.append(sends.start(w3, rwx.at[at.x], device))
    rwx[at.x] = w3[...]
    sends.recv(copies)
    g[at.c, at.z, 0] = ab[at.x] + jnp.sum(rx[...], axis=0)
    g[at.c, at.z, 1] = jnp.sum(rwx[...], axis=0)

    mine = g.at[at.c, at.z]
    sends.recv([sends.start(mine, mine, d) for _, _, d in at.along("z")])
    mine = g.at[at.c]
    sends.recv([sends.start(mine, mine, partner)])
    for c in range(2):
        for z in range(NZ):
            proj_out[c * 8 : (c + 1) * 8, z * 128 : (z + 1) * 128] = g[c, z, 0]
    for z in range(NZ):
        table_out[z] = g[0, z, 1]
    sends.finish()


def scatter(proj, table):
    tile = (8, 128)
    f32 = jnp.float32
    half = NX // 2
    copies = 2 + 3 * 7 + 3 * 7 + 2 * 3 + 7 + 1
    vmem = pl.BlockSpec(memory_space=pltpu.VMEM)
    return pl.pallas_call(
        scatter_kernel,
        out_shape=(
            jax.ShapeDtypeStruct((16, 1024), f32),
            jax.ShapeDtypeStruct((NZ,) + tile, f32),
        ),
        in_specs=[vmem, vmem],
        out_specs=(vmem, vmem),
        scratch_shapes=[
            pltpu.VMEM((NX, NY, 8, 1024), f32),
            pltpu.VMEM((NZ,) + tile, f32),
            pltpu.VMEM((NX, NY, NZ) + tile, f32),
            pltpu.VMEM((NZ,) + tile, f32),
            pltpu.VMEM((NZ - 1, half, NY) + tile, f32),
            pltpu.VMEM((NY - 1, half, NZ) + tile, f32),
            pltpu.VMEM((NZ - 1,) + tile, f32),
            pltpu.VMEM((half, NY) + tile, f32),
            pltpu.VMEM((half, NZ) + tile, f32),
            pltpu.VMEM(tile, f32),
            pltpu.VMEM((NY - 1, half) + tile, f32),
            pltpu.VMEM((NZ - 1, half) + tile, f32),
            pltpu.VMEM((NY,) + tile, f32),
            pltpu.VMEM((NX,) + tile, f32),
            pltpu.VMEM(tile, f32),
            pltpu.VMEM((NX - 1,) + tile, f32),
            pltpu.VMEM((NX,) + tile, f32),
            pltpu.VMEM((2, NZ, 2) + tile, f32),
            pltpu.SemaphoreType.DMA((copies,)),
            pltpu.SemaphoreType.DMA((copies,)),
        ],
        compiler_params=pltpu.CompilerParams(collective_id=2, has_side_effects=True),
        name="scatter",
    )(proj, table)


def body(
    vertex_inputs,
    partition_embed_matrix,
    selector_embed_matrix,
    partition_affinity_matrix,
    sharpness_divisor,
    latent_query_key_value_maps,
    result_cotangent,
):
    local_rows = vertex_inputs.shape[0]
    attn_group_index = sharpness_divisor.shape[0]
    head_width = partition_affinity_matrix.shape[0]
    slice_count = partition_affinity_matrix.shape[1]
    feature = jnp.dot(
        vertex_inputs, partition_embed_matrix, preferred_element_type=jnp.float32
    ).astype(jnp.bfloat16)
    middle = jnp.dot(
        vertex_inputs, selector_embed_matrix, preferred_element_type=jnp.float32
    ).astype(jnp.bfloat16)
    middle_heads = middle.reshape(local_rows, attn_group_index, head_width)
    feature_heads = feature.reshape(local_rows, attn_group_index, head_width)
    grad_heads = result_cotangent.reshape(local_rows, attn_group_index, head_width)
    unclamped_attention_affinity = jnp.einsum(
        "nhc,cg->nhg", middle_heads, partition_affinity_matrix, preferred_element_type=jnp.float32
    )
    smooth_clamping_function = jnp.tanh(
        unclamped_attention_affinity / (partition_affinity_bound * sharpness_divisor[None, :, None])
    )
    exp_logit = jnp.exp(partition_affinity_bound * smooth_clamping_function)
    weight = exp_logit / jnp.sum(exp_logit, axis=-1, keepdims=True)
    weight_b = weight.astype(jnp.bfloat16)
    mass_part = jnp.sum(weight, axis=0)
    both_heads = jnp.concatenate([feature_heads, grad_heads], axis=-1)
    both_part = jnp.einsum(
        "nhg,nhc->hgc", weight_b, both_heads, preferred_element_type=jnp.float32
    )
    full, slice_mass = total(
        both_part.reshape(2, NZ, NX, 8, 128),
        jnp.pad(mass_part, ((0, 0), (0, 128 - slice_count))),
    )
    full = full.reshape(attn_group_index, slice_count, 2 * head_width)
    denominator = slice_mass[:, :slice_count] + epsilon
    token_heads = full[:, :, :head_width]
    back_heads = full[:, :, head_width:]
    tokens = token_heads / denominator[:, :, None]
    out_token, pullback = jax.vjp(token_mix, tokens, latent_query_key_value_maps)
    grad_token, grad_w_token = pullback(back_heads)
    out_b = out_token.astype(jnp.bfloat16)
    grad_sum_b = (grad_token / denominator[:, :, None]).astype(jnp.bfloat16)
    grad_mass = -jnp.sum(grad_token * tokens, axis=-1) / denominator
    grad_weight = jnp.einsum("nhc,hgc->nhg", grad_heads, out_b, preferred_element_type=jnp.float32)
    grad_weight = grad_weight + jnp.einsum(
        "nhc,hgc->nhg", feature_heads, grad_sum_b, preferred_element_type=jnp.float32
    )
    grad_weight = grad_weight + grad_mass[None]
    preactivation_cotangent = weight * (
        grad_weight - jnp.sum(weight * grad_weight, axis=-1, keepdims=True)
    )
    unprocessed_cotangent = (
        preactivation_cotangent
        * (1.0 - smooth_clamping_function * smooth_clamping_function)
        / sharpness_divisor[None, :, None]
    ).astype(jnp.bfloat16)
    grad_feature = (
        jnp.einsum("nhg,hgc->nhc", weight_b, grad_sum_b, preferred_element_type=jnp.float32)
        .reshape(local_rows, attn_group_index * head_width)
        .astype(jnp.bfloat16)
    )
    grad_mid = (
        jnp.einsum(
            "nhg,cg->nhc",
            unprocessed_cotangent,
            partition_affinity_matrix,
            preferred_element_type=jnp.float32,
        )
        .reshape(local_rows, attn_group_index * head_width)
        .astype(jnp.bfloat16)
    )
    grad_points = jnp.dot(
        grad_feature, partition_embed_matrix.T, preferred_element_type=jnp.float32
    )
    grad_points = (
        grad_points + jnp.dot(grad_mid, selector_embed_matrix.T, preferred_element_type=jnp.float32)
    ).astype(jnp.bfloat16)
    grad_joined = jnp.concatenate([grad_feature, grad_mid], axis=1)
    slice_part = jnp.einsum(
        "nhc,nhg->cg", middle_heads, unprocessed_cotangent, preferred_element_type=jnp.float32
    )
    proj_part = lax.dot_general(
        vertex_inputs, grad_joined, (((0,), (0,)), ((), ())), preferred_element_type=jnp.float32
    )
    grad_proj, table = scatter(
        proj_part.reshape(NX, NY, 2, 8, 1024),
        jnp.pad(slice_part, ((0, 0), (0, 128 - slice_count))).reshape(NZ, 8, 128),
    )
    grad_w_slice = table.reshape(head_width, 128)[:, :slice_count]
    return (grad_points, grad_proj, grad_w_slice, grad_w_token)


def solution(mesh):
    return jax.shard_map(
        body,
        mesh=mesh,
        in_specs=(
            P(("region", "band"), None),
            P(),
            P(),
            P(),
            P(),
            P(),
            P(("region", "band"), None),
        ),
        out_specs=(P(("region", "band"), None), P("region", None), P(), P()),
        check_vma=False,
    )
```

```python
import math

import jax
import jax.numpy as jnp
from jax import lax
from jax.experimental import pallas as pl
from jax.experimental.pallas import tpu as pltpu
from jax.sharding import PartitionSpec as P

partition_affinity_bound = 8.0
score_cap = 10.0
epsilon = 1e-05

NX, NY, NZ = 4, 8, 8
MESH = pl.DeviceIdType.MESH


class Place:
    def __init__(self):
        region, band = lax.axis_index("region"), lax.axis_index("band")
        self.x, self.y = lax.div(region, NY), lax.rem(region, NY)
        self.z, self.c = lax.div(band, 2), lax.rem(band, 2)

    def device(self, x=None, y=None, z=None, c=None):
        x = self.x if x is None else x
        y = self.y if y is None else y
        z = self.z if z is None else z
        c = self.c if c is None else c
        return {"region": x * NY + y, "band": z * 2 + c}

    def along(self, axis):
        size = {"x": NX, "y": NY, "z": NZ}[axis]
        here = getattr(self, axis)
        order = sorted(range(1, size), key=lambda k: -min(k, size - k))
        for k in order:
            there = lax.rem(here + k, size)
            yield k, there, self.device(**{axis: there})

    def greet(self):
        barrier = pltpu.get_barrier_semaphore()
        count = 0
        partners = [self.device(c=1 - self.c)]
        for axis in "xyz":
            partners += [d for _, _, d in self.along(axis)]
        for d in partners:
            pl.semaphore_signal(barrier, inc=1, device_id=d, device_id_type=MESH)
            count += 1
        return lambda: pl.semaphore_wait(barrier, count)


class Sends:
    def __init__(self, send_sem, recv_sem):
        self.send_sem, self.recv_sem, self.used, self.open = send_sem, recv_sem, 0, []

    def start(self, src, dst, device):
        i = self.used
        self.used += 1
        copy = pltpu.make_async_remote_copy(
            src_ref=src,
            dst_ref=dst,
            send_sem=self.send_sem.at[i],
            recv_sem=self.recv_sem.at[i],
            device_id=device,
            device_id_type=MESH,
        )
        copy.start()
        self.open.append(copy)
        return copy

    def recv(self, copies):
        for copy in copies:
            copy.wait_recv()

    def finish(self):
        for copy in self.open:
            copy.wait_send()


HEADS, PAIRS, WIDTH = 8, 4, 64
LANES = 128
HIGHEST = lax.Precision.HIGHEST
F32, BF16 = jnp.float32, jnp.bfloat16


def dot(a, b, over=(1, 0), precision=None):
    dims = (((over[0],), (over[1],)), ((), ()))
    return lax.dot_general(a, b, dims, precision=precision, preferred_element_type=F32)


def exact(a, b, over=(1, 0)):
    return dot(a, b, over, HIGHEST)


def same_half(rows, lanes=LANES):
    r = lax.broadcasted_iota(jnp.int32, (rows, lanes), 0)
    l = lax.broadcasted_iota(jnp.int32, (rows, lanes), 1)
    return (r < WIDTH) == (l < WIDTH)


def swap(v):
    return pltpu.roll(v, WIDTH, 1)


def columns(p):
    return slice(p * LANES, (p + 1) * LANES)


def one_head(v, den, maps):
    tokens = v[:, :WIDTH] / den
    back = swap(v)[:, :WIDTH]
    q, k, w = (exact(tokens, maps[i]) for i in range(3))
    squash = jnp.tanh(exact(q, k, (1, 1)) / math.sqrt(WIDTH) / score_cap)
    e = jnp.exp(score_cap * squash)
    attention = e / jnp.sum(e, axis=1, keepdims=True)
    out = tokens + exact(attention, w)
    d_attention = exact(back, w, (1, 1))
    d_w = exact(attention, back, (0, 0))
    d_capped = attention * (
        d_attention - jnp.sum(d_attention * attention, axis=1, keepdims=True)
    )
    d_scores = d_capped * (1.0 - squash * squash) / math.sqrt(WIDTH)
    d_q = exact(d_scores, k)
    d_k = exact(d_scores, q, (0, 0))
    grad = back + exact(d_q, maps[0], (1, 1)) + exact(d_k, maps[1], (1, 1))
    grad = grad + exact(d_w, maps[2], (1, 1))
    grad_maps = [exact(tokens, d, (0, 0)) for d in (d_q, d_k, d_w)]
    grad_mass = -jnp.sum(grad * tokens, axis=1, keepdims=True) / den
    return out, grad / den, grad_mass, grad_maps


def placed(v, half):
    r = lax.broadcasted_iota(jnp.int32, (WIDTH, LANES), 0)
    l = lax.broadcasted_iota(jnp.int32, (WIDTH, LANES), 1)
    return exact(v, (l == r + half * WIDTH).astype(F32))


def kernel(
    x_ref, we_ref, ws_ref, wa_ref, sharp_ref, maps_ref, cot_ref,
    points_out, proj_out, slice_out, maps_out,
    feature, middle, weight, squash_ref, weight_b, part, mass, xt, table, gcat,
    rc, rcm, s1, m1, rz, rzm, s2, m2, rx, rxm, s3, ry, headbuf, res,
    proj, rcp, rcw, p1, w1, pz, py, wz, a2, b2, w2, py2, pz2, wy, ab, w3, px, wx, g, gt,
    send_sem, recv_sem,
):
    at = Place()
    greeted = at.greet()
    sends = Sends(send_sem, recv_sem)
    other = 1 - at.c
    partner = at.device(c=other)
    half_mask = same_half(LANES)
    ones = half_mask.astype(F32)
    lane_low = lax.broadcasted_iota(jnp.int32, (1, LANES), 1) < WIDTH

    wa = wa_ref[...]
    wa_pair = jnp.where(half_mask, wa, jnp.zeros_like(wa))

    def sharp(p):
        return jnp.where(lane_low, sharp_ref[2 * p], sharp_ref[2 * p + 1])

    feature[...] = dot(x_ref[...], we_ref[...]).astype(BF16)
    middle[...] = dot(x_ref[...], ws_ref[...]).astype(BF16)
    mass[...] = jnp.zeros_like(mass)
    for p in range(PAIRS):
        cols = columns(p)
        raw = dot(middle[:, cols], wa_pair)
        squash = jnp.tanh(raw / (partition_affinity_bound * sharp(p)))
        e = jnp.exp(partition_affinity_bound * squash)
        w = e / exact(e, ones)
        wb = w.astype(BF16)
        squash_ref[:, cols] = squash
        weight[:, cols] = w
        weight_b[:, cols] = wb
        mass[p : p + 1, :] = jnp.sum(w, axis=0, keepdims=True)
        tok = dot(wb, feature[:, cols], (0, 0))
        back = dot(wb, cot_ref[:, cols], (0, 0))
        both = jnp.where(half_mask, tok, swap(back))
        part[p // 2, 4 * (p % 2) : 4 * (p % 2) + 4] = both.reshape(4, NX, 8, LANES)

    greeted()
    copies = [
        sends.start(part.at[other], rc, partner),
        sends.start(mass, rcm, partner),
    ]
    xt[...] = x_ref[...].T
    sends.recv(copies)
    s1[...] = part[at.c] + rc[...]
    m1[...] = mass[...] + rcm[...]

    copies = []
    for k, there, device in at.along("z"):
        copies.append(sends.start(s1.at[there], rz.at[k - 1], device))
        copies.append(sends.start(m1, rzm.at[at.z], device))
    rzm[at.z] = m1[...]
    sends.recv(copies)
    s2[...] = s1[at.z] + jnp.sum(rz[...], axis=0)
    m2[...] = jnp.sum(rzm[...], axis=0)

    copies = []
    for k, there, device in at.along("x"):
        copies.append(sends.start(s2.at[there], rx.at[k - 1], device))
        copies.append(sends.start(m2, rxm.at[at.x], device))
    rxm[at.x] = m2[...]
    sends.recv(copies)
    s3[0] = s2[at.x] + jnp.sum(rx[...], axis=0)
    s3[1] = jnp.sum(rxm[...], axis=0)

    copies = []
    for k, there, device in at.along("y"):
        copies.append(sends.start(s3, ry.at[at.y], device))
    ry[at.y] = s3[...]
    sends.recv(copies)
    done = jnp.sum(ry[...], axis=0)

    zpair, zside = lax.div(at.z, 2), lax.rem(at.z, 2)
    headbuf[zside, at.x] = done[0]
    mine = headbuf.at[zside, at.x]
    sends.recv([sends.start(mine, mine, d) for _, _, d in at.along("x")])
    mine = headbuf.at[zside]
    sends.recv([sends.start(mine, mine, at.device(z=zpair * 2 + 1 - zside))])

    odd = lax.rem(zpair, 2)
    pair = at.c * 2 + lax.div(zpair, 2)
    rows8 = lax.broadcasted_iota(jnp.int32, (8, LANES), 0)
    mass_row = jnp.sum(jnp.where(rows8 == pair, done[1], 0.0), axis=0, keepdims=True)
    r = lax.broadcasted_iota(jnp.int32, (WIDTH, LANES), 0)
    l = lax.broadcasted_iota(jnp.int32, (WIDTH, LANES), 1)
    den = jnp.sum(jnp.where(l == r + odd * WIDTH, mass_row, 0.0), axis=1, keepdims=True)
    v = headbuf[...].reshape(WIDTH, LANES)
    v = jnp.where(odd == 1, swap(v), v)
    out, grad_sum, grad_mass, grad_maps = one_head(v, den + epsilon, maps_ref)
    both = placed(grad_sum, 0) + placed(out, 1)
    both = jnp.where(odd == 1, swap(both), both)
    res[at.c, zpair, :, pl.ds(0, 4)] = both.reshape(2, 4, 8, LANES)
    mass_row = jnp.sum(
        jnp.where((l == r) | (l == r + WIDTH), grad_mass, 0.0), axis=0, keepdims=True
    )
    for side in range(2):
        res[at.c, zpair, side, 4] = jnp.broadcast_to(mass_row, (8, LANES))

    mine = res.at[at.c, zpair, zside]
    copies = []
    for k in range(1, 4):
        for s in range(2):
            there = lax.rem(zpair + k, 4) * 2 + lax.rem(zside + s, 2)
            copies.append(sends.start(mine, mine, at.device(z=there)))
    scale = 1.0 / (NX * NY * 2)
    table_low = placed(grad_maps[0] * scale, 1)
    table_high = placed(grad_maps[1] * scale, 0) + placed(grad_maps[2] * scale, 1)
    sends.recv(copies)
    mine = res.at[at.c]
    sends.recv([sends.start(mine, mine, partner)])

    slice_acc = jnp.zeros((LANES, LANES), F32)
    for p in range(PAIRS):
        cols = columns(p)
        c, z0 = p // 2, (p % 2) * 2
        v = res[c, z0 : z0 + 2, :, 0:4].reshape(LANES, LANES)
        gm = jnp.where(lane_low, res[c, z0, 0, 4, 0:1], res[c, z0 + 1, 0, 4, 0:1])
        gs = jnp.where(half_mask, v, 0.0).astype(BF16)
        ob = jnp.where(half_mask, swap(v), 0.0).astype(BF16)
        gw = dot(cot_ref[:, cols], ob, (1, 1)) + dot(feature[:, cols], gs, (1, 1)) + gm
        w = weight[:, cols]
        squash = squash_ref[:, cols]
        pre = w * (gw - exact(w * gw, ones))
        gr = (pre * (1.0 - squash * squash) / sharp(p)).astype(BF16)
        gcat[p] = dot(weight_b[:, cols], gs).astype(BF16)
        gcat[PAIRS + p] = dot(gr, wa_pair, (1, 1)).astype(BF16)
        slice_acc = slice_acc + dot(middle[:, cols], gr, (0, 0))

    core_copies = []
    order = [k for k, _, _ in at.along("z")] + [0]
    for k in order:
        blk = lax.rem(at.z + k, NZ)
        r = dot(xt[...], gcat[blk]).reshape(NX, NY, 2, 8, LANES)
        for c in range(2):
            proj[c, blk] = r[:, :, c]
        core_copies.append(sends.start(proj.at[other, blk], rcp.at[blk], partner))
    sl = slice_acc[:WIDTH] + swap(slice_acc[WIDTH:])
    sl = jnp.where(lane_low, sl, 0.0)
    table[:, 0] = (sl + table_low).reshape(NZ, 8, LANES)
    table[:, 1] = table_high.reshape(NZ, 8, LANES)
    table_copy = sends.start(table, rcw, partner)

    half = NX // 2
    z_of = {k: d for k, _, d in at.along("z")}
    copies = []
    for k, copy in zip(order, core_copies):
        blk = lax.rem(at.z + k, NZ)
        copy.wait_recv()
        p1[blk] = proj[at.c, blk] + rcp[blk]
        if k:
            copies.append(sends.start(p1.at[blk, pl.ds(0, half)], pz.at[k - 1], z_of[k]))
    for k, yt, yd in at.along("y"):
        copies.append(sends.start(p1.at[:, pl.ds(half, half), yt], py.at[k - 1], yd))
    table_copy.wait_recv()
    w1[...] = table[...] + rcw[...]
    for k, zt, zd in at.along("z"):
        copies.append(sends.start(w1.at[zt], wz.at[k - 1], zd))

    points = jnp.zeros(points_out.shape, F32)
    for p in range(PAIRS):
        cols = columns(p)
        points = points + dot(gcat[p], we_ref[:, cols], (1, 1))
    for p in range(PAIRS):
        cols = columns(p)
        points = points + dot(gcat[PAIRS + p], ws_ref[:, cols], (1, 1))
    points_out[...] = points.astype(BF16)

    sends.recv(copies)
    a2[...] = p1[at.z, pl.ds(0, half)] + jnp.sum(pz[...], axis=0)
    b2[...] = p1[:, pl.ds(half, half), at.y] + jnp.sum(py[...], axis=0)
    w2[...] = w1[at.z] + jnp.sum(wz[...], axis=0)

    copies = []
    for (k, zt, zd), (_, yt, yd) in zip(at.along("z"), at.along("y")):
        copies.append(sends.start(a2.at[:, yt], py2.at[k - 1], yd))
        copies.append(sends.start(b2.at[zt], pz2.at[k - 1], zd))
        copies.append(sends.start(w2, wy.at[at.y], yd))
    wy[at.y] = w2[...]
    sends.recv(copies)
    ab[pl.ds(0, half)] = a2[:, at.y] + jnp.sum(py2[...], axis=0)
    ab[pl.ds(half, half)] = b2[at.z] + jnp.sum(pz2[...], axis=0)
    w3[...] = jnp.sum(wy[...], axis=0)

    copies = []
    for k, there, device in at.along("x"):
        copies.append(sends.start(ab.at[there], px.at[k - 1], device))
        copies.append(sends.start(w3, wx.at[at.x], device))
    wx[at.x] = w3[...]
    sends.recv(copies)
    g[at.c, at.z] = ab[at.x] + jnp.sum(px[...], axis=0)
    gt[at.z] = jnp.sum(wx[...], axis=0)

    mine, also = g.at[at.c, at.z], gt.at[at.z]
    copies = []
    for _, _, d in at.along("z"):
        copies.append(sends.start(mine, mine, d))
        copies.append(sends.start(also, also, d))
    sends.recv(copies)
    mine = g.at[at.c]
    copies = [sends.start(mine, mine, partner)]
    low = gt[:, 0].reshape(WIDTH, LANES)
    high = gt[:, 1].reshape(WIDTH, LANES)
    slice_out[...] = low[:, :WIDTH]
    maps_out[0] = swap(low)[:, :WIDTH]
    maps_out[1] = high[:, :WIDTH]
    maps_out[2] = swap(high)[:, :WIDTH]
    sends.recv(copies)
    for c in range(2):
        for z in range(NZ):
            proj_out[c * 8 : (c + 1) * 8, columns(z)] = g[c, z]
    sends.finish()


def body(
    vertex_inputs,
    partition_embed_matrix,
    selector_embed_matrix,
    partition_affinity_matrix,
    sharpness_divisor,
    latent_query_key_value_maps,
    result_cotangent,
):
    rows, width = vertex_inputs.shape
    tile = (8, LANES)
    half = NX // 2
    copies = 2 + 2 * 7 + 2 * 3 + 7 + 3 + 1 + 6 + 1 + 8 + 1 + 3 * 7 + 3 * 7 + 2 * 3 + 2 * 7 + 1
    vmem = pl.BlockSpec(memory_space=pltpu.VMEM)
    smem = pl.BlockSpec(memory_space=pltpu.SMEM)

    def f32(*shape):
        return pltpu.VMEM(shape + tile, F32)

    return pl.pallas_call(
        kernel,
        out_shape=(
            jax.ShapeDtypeStruct((rows, width), BF16),
            jax.ShapeDtypeStruct((16, 1024), F32),
            jax.ShapeDtypeStruct((WIDTH, WIDTH), F32),
            jax.ShapeDtypeStruct((3, WIDTH, WIDTH), F32),
        ),
        in_specs=[vmem, vmem, vmem, vmem, smem, vmem, vmem],
        out_specs=(vmem, vmem, vmem, vmem),
        scratch_shapes=[
            pltpu.VMEM((rows, width), BF16),
            pltpu.VMEM((rows, width), BF16),
            pltpu.VMEM((rows, width), F32),
            pltpu.VMEM((rows, width), F32),
            pltpu.VMEM((rows, width), BF16),
            f32(2, NZ, NX),
            f32(),
            pltpu.VMEM((width, rows), BF16),
            f32(NZ, 2),
            pltpu.VMEM((NZ, rows, LANES), BF16),
            f32(NZ, NX),
            f32(),
            f32(NZ, NX),
            f32(),
            f32(NZ - 1, NX),
            f32(NZ),
            f32(NX),
            f32(),
            f32(NX - 1),
            f32(NX),
            f32(2),
            f32(NY, 2),
            f32(2, NX),
            f32(2, 4, 2, 5),
            f32(2, NZ, NX, NY),
            f32(NZ, NX, NY),
            f32(NZ, 2),
            f32(NZ, NX, NY),
            f32(NZ, 2),
            f32(NZ - 1, half, NY),
            f32(NY - 1, NZ, half),
            f32(NZ - 1, 2),
            f32(half, NY),
            f32(NZ, half),
            f32(2),
            f32(NY - 1, half),
            f32(NZ - 1, half),
            f32(NY, 2),
            f32(NX),
            f32(2),
            f32(NX - 1),
            f32(NX, 2),
            f32(2, NZ),
            f32(NZ, 2),
            pltpu.SemaphoreType.DMA((copies,)),
            pltpu.SemaphoreType.DMA((copies,)),
        ],
        compiler_params=pltpu.CompilerParams(collective_id=1, has_side_effects=True),
        name="layer",
    )(
        vertex_inputs,
        partition_embed_matrix,
        selector_embed_matrix,
        jnp.tile(partition_affinity_matrix, (2, 2)),
        sharpness_divisor,
        latent_query_key_value_maps,
        result_cotangent,
    )


def solution(mesh):
    return jax.shard_map(
        body,
        mesh=mesh,
        in_specs=(
            P(("region", "band"), None),
            P(),
            P(),
            P(),
            P(),
            P(),
            P(("region", "band"), None),
        ),
        out_specs=(P(("region", "band"), None), P("region", None), P(), P()),
        check_vma=False,
    )
```

```python
import math

import jax
import jax.numpy as jnp
from jax import lax
from jax.experimental import pallas as pl
from jax.experimental.pallas import tpu as pltpu
from jax.sharding import PartitionSpec as P

partition_affinity_bound = 8.0
score_cap = 10.0
epsilon = 1e-05

NX, NY, NZ = 4, 8, 8
MESH = pl.DeviceIdType.MESH


class Place:
    def __init__(self):
        region, band = lax.axis_index("region"), lax.axis_index("band")
        self.x, self.y = lax.div(region, NY), lax.rem(region, NY)
        self.z, self.c = lax.div(band, 2), lax.rem(band, 2)

    def device(self, x=None, y=None, z=None, c=None):
        x = self.x if x is None else x
        y = self.y if y is None else y
        z = self.z if z is None else z
        c = self.c if c is None else c
        return {"region": x * NY + y, "band": z * 2 + c}

    def along(self, axis):
        size = {"x": NX, "y": NY, "z": NZ}[axis]
        here = getattr(self, axis)
        order = sorted(range(1, size), key=lambda k: -min(k, size - k))
        for k in order:
            there = lax.rem(here + k, size)
            yield k, there, self.device(**{axis: there})

    def greet(self):
        barrier = pltpu.get_barrier_semaphore()
        count = 0
        partners = [self.device(c=1 - self.c)]
        for axis in "xyz":
            partners += [d for _, _, d in self.along(axis)]
        for d in partners:
            pl.semaphore_signal(barrier, inc=1, device_id=d, device_id_type=MESH)
            count += 1
        return lambda: pl.semaphore_wait(barrier, count)


class Sends:
    def __init__(self, send_sem, recv_sem):
        self.send_sem, self.recv_sem, self.used, self.open = send_sem, recv_sem, 0, []

    def start(self, src, dst, device):
        i = self.used
        self.used += 1
        copy = pltpu.make_async_remote_copy(
            src_ref=src,
            dst_ref=dst,
            send_sem=self.send_sem.at[i],
            recv_sem=self.recv_sem.at[i],
            device_id=device,
            device_id_type=MESH,
        )
        copy.start()
        self.open.append(copy)
        return copy

    def recv(self, copies):
        for copy in copies:
            copy.wait_recv()

    def finish(self):
        for copy in self.open:
            copy.wait_send()


HEADS, PAIRS, WIDTH = 8, 4, 64
LANES = 128
HIGHEST = lax.Precision.HIGHEST
F32, BF16 = jnp.float32, jnp.bfloat16


def dot(a, b, over=(1, 0), precision=None):
    dims = (((over[0],), (over[1],)), ((), ()))
    return lax.dot_general(a, b, dims, precision=precision, preferred_element_type=F32)


def exact(a, b, over=(1, 0)):
    return dot(a, b, over, HIGHEST)


def same_half(rows, lanes=LANES):
    r = lax.broadcasted_iota(jnp.int32, (rows, lanes), 0)
    l = lax.broadcasted_iota(jnp.int32, (rows, lanes), 1)
    return (r < WIDTH) == (l < WIDTH)


def swap(v):
    return pltpu.roll(v, WIDTH, 1)


def columns(p):
    return slice(p * LANES, (p + 1) * LANES)


def one_head(v, den, maps):
    tokens = v[:, :WIDTH] / den
    back = swap(v)[:, :WIDTH]
    q, k, w = (exact(tokens, maps[i]) for i in range(3))
    squash = jnp.tanh(exact(q, k, (1, 1)) / math.sqrt(WIDTH) / score_cap)
    e = jnp.exp(score_cap * squash)
    attention = e / jnp.sum(e, axis=1, keepdims=True)
    out = tokens + exact(attention, w)
    d_attention = exact(back, w, (1, 1))
    d_w = exact(attention, back, (0, 0))
    d_capped = attention * (
        d_attention - jnp.sum(d_attention * attention, axis=1, keepdims=True)
    )
    d_scores = d_capped * (1.0 - squash * squash) / math.sqrt(WIDTH)
    d_q = exact(d_scores, k)
    d_k = exact(d_scores, q, (0, 0))
    grad = back + exact(d_q, maps[0], (1, 1)) + exact(d_k, maps[1], (1, 1))
    grad = grad + exact(d_w, maps[2], (1, 1))
    grad_maps = [exact(tokens, d, (0, 0)) for d in (d_q, d_k, d_w)]
    grad_mass = -jnp.sum(grad * tokens, axis=1, keepdims=True) / den
    return out, grad / den, grad_mass, grad_maps


def placed(v, half):
    r = lax.broadcasted_iota(jnp.int32, (WIDTH, LANES), 0)
    l = lax.broadcasted_iota(jnp.int32, (WIDTH, LANES), 1)
    return exact(v, (l == r + half * WIDTH).astype(F32))


def kernel(
    x_ref, we_ref, ws_ref, wa_ref, sharp_ref, maps_ref, cot_ref,
    points_out, proj_out, slice_out, maps_out,
    feature, middle, weight, squash_ref, weight_b, part, mass, xt, table, gcat,
    rc, rcm, s1, m1, rz, rzm, s2, m2, rx, rxm, s3, ry, headbuf, res,
    proj, rcp, rcw, p1, w1, pz, py, wz, a2, b2, w2, py2, pz2, wy, ab, w3, px, wx, g, gt,
    send_sem, recv_sem,
):
    at = Place()
    greeted = at.greet()
    sends = Sends(send_sem, recv_sem)
    other = 1 - at.c
    partner = at.device(c=other)
    half_mask = same_half(LANES)
    ones = half_mask.astype(F32)
    lane_low = lax.broadcasted_iota(jnp.int32, (1, LANES), 1) < WIDTH

    r = lax.broadcasted_iota(jnp.int32, (LANES, WIDTH), 0)
    l = lax.broadcasted_iota(jnp.int32, (LANES, WIDTH), 1)
    twice = ((l == r) | (l == r - WIDTH)).astype(BF16)
    wa_pair = dot(dot(twice, wa_ref[...]).astype(BF16), twice, (1, 1))
    wa_pair = jnp.where(half_mask, wa_pair, 0.0).astype(BF16)

    def sharp(p):
        return jnp.where(lane_low, sharp_ref[2 * p], sharp_ref[2 * p + 1])

    feature[...] = dot(x_ref[...], we_ref[...]).astype(BF16)
    middle[...] = dot(x_ref[...], ws_ref[...]).astype(BF16)
    mass[...] = jnp.zeros_like(mass)
    for p in range(PAIRS):
        cols = columns(p)
        raw = dot(middle[:, cols], wa_pair)
        squash = jnp.tanh(raw / (partition_affinity_bound * sharp(p)))
        e = jnp.exp(partition_affinity_bound * squash)
        w = e / exact(e, ones)
        wb = w.astype(BF16)
        squash_ref[:, cols] = squash
        weight[:, cols] = w
        weight_b[:, cols] = wb
        mass[p : p + 1, :] = jnp.sum(w, axis=0, keepdims=True)
        tok = dot(wb, feature[:, cols], (0, 0))
        back = dot(wb, cot_ref[:, cols], (0, 0))
        both = jnp.where(half_mask, tok, swap(back))
        part[p // 2, 2 * (p % 2) : 2 * (p % 2) + 2] = both.reshape(2, NZ, 8, LANES)

    greeted()
    copies = [
        sends.start(part.at[other], rc, partner),
        sends.start(mass, rcm, partner),
    ]
    xt[...] = x_ref[...].T
    sends.recv(copies)
    s1[...] = part[at.c] + rc[...]
    m1[...] = mass[...] + rcm[...]

    copies = []
    for k, there, device in at.along("x"):
        copies.append(sends.start(s1.at[there], rx.at[k - 1], device))
        copies.append(sends.start(m1, rxm.at[at.x], device))
    rxm[at.x] = m1[...]
    sends.recv(copies)
    s2[...] = s1[at.x] + jnp.sum(rx[...], axis=0)
    m2[...] = jnp.sum(rxm[...], axis=0)

    copies = []
    for k, there, device in at.along("z"):
        copies.append(sends.start(s2.at[there], rz.at[k - 1], device))
        copies.append(sends.start(m2, rzm.at[at.z], device))
    rzm[at.z] = m2[...]
    sends.recv(copies)
    s3[0] = s2[at.z] + jnp.sum(rz[...], axis=0)
    s3[1] = jnp.sum(rzm[...], axis=0)

    copies = []
    for k, there, device in at.along("y"):
        copies.append(sends.start(s3, ry.at[at.y], device))
    ry[at.y] = s3[...]
    sends.recv(copies)
    done = jnp.sum(ry[...], axis=0)

    headbuf[at.z] = done[0]
    mine = headbuf.at[at.z]
    sends.recv([sends.start(mine, mine, d) for _, _, d in at.along("z")])

    odd = lax.rem(at.x, 2)
    pair = at.c * 2 + lax.div(at.x, 2)
    rows8 = lax.broadcasted_iota(jnp.int32, (8, LANES), 0)
    mass_row = jnp.sum(jnp.where(rows8 == pair, done[1], 0.0), axis=0, keepdims=True)
    r = lax.broadcasted_iota(jnp.int32, (WIDTH, LANES), 0)
    l = lax.broadcasted_iota(jnp.int32, (WIDTH, LANES), 1)
    den = jnp.sum(jnp.where(l == r + odd * WIDTH, mass_row, 0.0), axis=1, keepdims=True)
    v = headbuf[...].reshape(WIDTH, LANES)
    v = jnp.where(odd == 1, swap(v), v)
    out, grad_sum, grad_mass, grad_maps = one_head(v, den + epsilon, maps_ref)
    both = placed(grad_sum, 0) + placed(out, 1)
    both = jnp.where(odd == 1, swap(both), both)
    res[at.c, at.x, pl.ds(0, NZ)] = both.reshape(NZ, 8, LANES)
    mass_row = jnp.sum(
        jnp.where((l == r) | (l == r + WIDTH), grad_mass, 0.0), axis=0, keepdims=True
    )
    res[at.c, at.x, NZ] = jnp.broadcast_to(mass_row, (8, LANES))

    mine = res.at[at.c, at.x]
    copies = [(k, sends.start(mine, mine, d)) for k, _, d in at.along("x")]
    passed = [sends.start(mine, mine, partner)]
    scale = 1.0 / (NY * NZ)
    table_low = placed(grad_maps[0] * scale, 1)
    table_high = placed(grad_maps[1] * scale, 0) + placed(grad_maps[2] * scale, 1)
    for k, copy in copies:
        copy.wait_recv()
        came = res.at[at.c, lax.rem(at.x + NX - k, NX)]
        passed.append(sends.start(came, came, partner))
    sends.recv(passed)

    slice_acc = jnp.zeros((LANES, LANES), F32)
    for p in range(PAIRS):
        cols = columns(p)
        c, x0 = p // 2, (p % 2) * 2
        v = res[c, x0 : x0 + 2, 0:NZ].reshape(LANES, LANES)
        gm = jnp.where(lane_low, res[c, x0, NZ, 0:1], res[c, x0 + 1, NZ, 0:1])
        gs = jnp.where(half_mask, v, 0.0).astype(BF16)
        ob = jnp.where(half_mask, swap(v), 0.0).astype(BF16)
        gw = dot(cot_ref[:, cols], ob, (1, 1)) + dot(feature[:, cols], gs, (1, 1)) + gm
        w = weight[:, cols]
        squash = squash_ref[:, cols]
        pre = w * (gw - exact(w * gw, ones))
        gr = (pre * (1.0 - squash * squash) / sharp(p)).astype(BF16)
        gcat[p] = dot(weight_b[:, cols], gs).astype(BF16)
        gcat[PAIRS + p] = dot(gr, wa_pair, (1, 1)).astype(BF16)
        slice_acc = slice_acc + dot(middle[:, cols], gr, (0, 0))

    core_copies = []
    order = [k for k, _, _ in at.along("z")] + [0]
    for k in order:
        blk = lax.rem(at.z + k, NZ)
        r = dot(xt[...], gcat[blk]).reshape(NX, NY, 2, 8, LANES)
        for c in range(2):
            proj[c, blk] = r[:, :, c]
        core_copies.append(sends.start(proj.at[other, blk], rcp.at[blk], partner))
    sl = slice_acc[:WIDTH] + swap(slice_acc[WIDTH:])
    sl = jnp.where(lane_low, sl, 0.0)
    table[:, 0] = (sl + table_low).reshape(NZ, 8, LANES)
    table[:, 1] = table_high.reshape(NZ, 8, LANES)
    table_copy = sends.start(table, rcw, partner)

    half = NX // 2
    z_of = {k: d for k, _, d in at.along("z")}
    copies = []
    for k, copy in zip(order, core_copies):
        blk = lax.rem(at.z + k, NZ)
        copy.wait_recv()
        p1[blk] = proj[at.c, blk] + rcp[blk]
        if k:
            copies.append(sends.start(p1.at[blk, pl.ds(0, half)], pz.at[k - 1], z_of[k]))
        for j, yt, yd in at.along("y"):
            copies.append(sends.start(p1.at[blk, pl.ds(half, half), yt], py.at[j - 1, blk], yd))
    table_copy.wait_recv()
    w1[...] = table[...] + rcw[...]
    for k, zt, zd in at.along("z"):
        copies.append(sends.start(w1.at[zt], wz.at[k - 1], zd))

    points = jnp.zeros(points_out.shape, F32)
    for p in range(PAIRS):
        cols = columns(p)
        points = points + dot(gcat[p], we_ref[:, cols], (1, 1))
    for p in range(PAIRS):
        cols = columns(p)
        points = points + dot(gcat[PAIRS + p], ws_ref[:, cols], (1, 1))
    points_out[...] = points.astype(BF16)

    sends.recv(copies)
    a2[...] = p1[at.z, pl.ds(0, half)] + jnp.sum(pz[...], axis=0)
    b2[...] = p1[:, pl.ds(half, half), at.y] + jnp.sum(py[...], axis=0)
    w2[...] = w1[at.z] + jnp.sum(wz[...], axis=0)

    copies = []
    for (k, zt, zd), (_, yt, yd) in zip(at.along("z"), at.along("y")):
        copies.append(sends.start(a2.at[:, yt], py2.at[k - 1], yd))
        copies.append(sends.start(b2.at[zt], pz2.at[k - 1], zd))
        copies.append(sends.start(w2, wy.at[at.y], yd))
    wy[at.y] = w2[...]
    sends.recv(copies)
    ab[pl.ds(0, half)] = a2[:, at.y] + jnp.sum(py2[...], axis=0)
    ab[pl.ds(half, half)] = b2[at.z] + jnp.sum(pz2[...], axis=0)
    w3[...] = jnp.sum(wy[...], axis=0)

    copies = []
    for k, there, device in at.along("x"):
        copies.append(sends.start(ab.at[there], px.at[k - 1], device))
        copies.append(sends.start(w3, wx.at[at.x], device))
    wx[at.x] = w3[...]
    sends.recv(copies)
    g[at.c, at.z] = ab[at.x] + jnp.sum(px[...], axis=0)
    gt[at.z] = jnp.sum(wx[...], axis=0)

    mine, also = g.at[at.c, at.z], gt.at[at.z]
    copies = []
    for _, _, d in at.along("z"):
        copies.append(sends.start(mine, mine, d))
        copies.append(sends.start(also, also, d))
    sends.recv(copies)
    mine = g.at[at.c]
    copies = [sends.start(mine, mine, partner)]
    low = gt[:, 0].reshape(WIDTH, LANES)
    high = gt[:, 1].reshape(WIDTH, LANES)
    slice_out[...] = low[:, :WIDTH]
    maps_out[0] = swap(low)[:, :WIDTH]
    maps_out[1] = high[:, :WIDTH]
    maps_out[2] = swap(high)[:, :WIDTH]
    sends.recv(copies)
    for c in range(2):
        for z in range(NZ):
            proj_out[c * 8 : (c + 1) * 8, columns(z)] = g[c, z]
    sends.finish()


def store_kernel(*refs):
    sem = refs[8]
    copies = [pltpu.make_async_copy(refs[i], refs[4 + i], sem.at[i]) for i in range(4)]
    for copy in copies:
        copy.start()
    for copy in copies:
        copy.wait()


def body(
    vertex_inputs,
    partition_embed_matrix,
    selector_embed_matrix,
    partition_affinity_matrix,
    sharpness_divisor,
    latent_query_key_value_maps,
    result_cotangent,
):
    rows, width = vertex_inputs.shape
    tile = (8, LANES)
    half = NX // 2
    copies = 2 + 2 * 3 + 2 * 7 + 7 + 7 + 3 + 4 + 8 + 1 + 7 + 8 * 7 + 7 + 3 * 7 + 2 * 3 + 2 * 7 + 1
    vmem = pl.BlockSpec(memory_space=pltpu.VMEM)
    smem = pl.BlockSpec(memory_space=pltpu.SMEM)

    def f32(*shape):
        return pltpu.VMEM(shape + tile, F32)

    results = pl.pallas_call(
        kernel,
        out_shape=(
            jax.ShapeDtypeStruct((rows, width), BF16),
            jax.ShapeDtypeStruct((16, 1024), F32),
            jax.ShapeDtypeStruct((WIDTH, WIDTH), F32),
            jax.ShapeDtypeStruct((3, WIDTH, WIDTH), F32),
        ),
        in_specs=[vmem, vmem, vmem, vmem, smem, vmem, vmem],
        out_specs=(vmem, vmem, vmem, vmem),
        scratch_shapes=[
            pltpu.VMEM((rows, width), BF16),
            pltpu.VMEM((rows, width), BF16),
            pltpu.VMEM((rows, width), F32),
            pltpu.VMEM((rows, width), F32),
            pltpu.VMEM((rows, width), BF16),
            f32(2, NX, NZ),
            f32(),
            pltpu.VMEM((width, rows), BF16),
            f32(NZ, 2),
            pltpu.VMEM((NZ, rows, LANES), BF16),
            f32(NX, NZ),
            f32(),
            f32(NX, NZ),
            f32(),
            f32(NZ - 1),
            f32(NZ),
            f32(NZ),
            f32(),
            f32(NX - 1, NZ),
            f32(NX),
            f32(2),
            f32(NY, 2),
            f32(NZ),
            f32(2, NX, NZ + 1),
            f32(2, NZ, NX, NY),
            f32(NZ, NX, NY),
            f32(NZ, 2),
            f32(NZ, NX, NY),
            f32(NZ, 2),
            f32(NZ - 1, half, NY),
            f32(NY - 1, NZ, half),
            f32(NZ - 1, 2),
            f32(half, NY),
            f32(NZ, half),
            f32(2),
            f32(NY - 1, half),
            f32(NZ - 1, half),
            f32(NY, 2),
            f32(NX),
            f32(2),
            f32(NX - 1),
            f32(NX, 2),
            f32(2, NZ),
            f32(NZ, 2),
            pltpu.SemaphoreType.DMA((copies,)),
            pltpu.SemaphoreType.DMA((copies,)),
        ],
        compiler_params=pltpu.CompilerParams(collective_id=1, has_side_effects=True),
        name="layer",
    )(
        vertex_inputs,
        partition_embed_matrix,
        selector_embed_matrix,
        partition_affinity_matrix,
        sharpness_divisor,
        latent_query_key_value_maps,
        result_cotangent,
    )
    return pl.pallas_call(
        store_kernel,
        out_shape=tuple(jax.ShapeDtypeStruct(r.shape, r.dtype) for r in results),
        in_specs=[vmem] * 4,
        out_specs=(pl.BlockSpec(memory_space=pl.ANY),) * 4,
        scratch_shapes=[pltpu.SemaphoreType.DMA((4,))],
        name="store",
    )(*results)


def solution(mesh):
    return jax.shard_map(
        body,
        mesh=mesh,
        in_specs=(
            P(("region", "band"), None),
            P(),
            P(),
            P(),
            P(),
            P(),
            P(("region", "band"), None),
        ),
        out_specs=(P(("region", "band"), None), P("region", None), P(), P()),
        check_vma=False,
    )
```

```python
import math

import jax
import jax.numpy as jnp
from jax import lax
from jax.experimental import pallas as pl
from jax.experimental.pallas import tpu as pltpu
from jax.sharding import PartitionSpec as P

partition_affinity_bound = 8.0
score_cap = 10.0
epsilon = 1e-05

NX, NY, NZ = 4, 8, 8
MESH = pl.DeviceIdType.MESH


class Place:
    def __init__(self):
        region, band = lax.axis_index("region"), lax.axis_index("band")
        self.x, self.y = lax.div(region, NY), lax.rem(region, NY)
        self.z, self.c = lax.div(band, 2), lax.rem(band, 2)

    def device(self, x=None, y=None, z=None, c=None):
        x = self.x if x is None else x
        y = self.y if y is None else y
        z = self.z if z is None else z
        c = self.c if c is None else c
        return {"region": x * NY + y, "band": z * 2 + c}

    def along(self, axis):
        size = {"x": NX, "y": NY, "z": NZ}[axis]
        here = getattr(self, axis)
        order = sorted(range(1, size), key=lambda k: -min(k, size - k))
        for k in order:
            there = lax.rem(here + k, size)
            yield k, there, self.device(**{axis: there})

    def greet(self):
        barrier = pltpu.get_barrier_semaphore()
        count = 0
        partners = [self.device(c=1 - self.c)]
        for axis in "xyz":
            partners += [d for _, _, d in self.along(axis)]
        for d in partners:
            pl.semaphore_signal(barrier, inc=1, device_id=d, device_id_type=MESH)
            count += 1
        return lambda: pl.semaphore_wait(barrier, count)


class Sends:
    def __init__(self, send_sem, recv_sem):
        self.send_sem, self.recv_sem, self.used, self.open = send_sem, recv_sem, 0, []

    def plan(self, src, dst, device):
        i = self.used
        self.used += 1
        return pltpu.make_async_remote_copy(
            src_ref=src,
            dst_ref=dst,
            send_sem=self.send_sem.at[i],
            recv_sem=self.recv_sem.at[i],
            device_id=device,
            device_id_type=MESH,
        )

    def start(self, src, dst, device):
        copy = self.plan(src, dst, device)
        copy.start()
        self.open.append(copy)
        return copy

    def recv(self, copies):
        for copy in copies:
            copy.wait_recv()

    def finish(self):
        for copy in self.open:
            copy.wait_send()


HEADS, PAIRS, WIDTH = 8, 4, 64
LANES = 128
HIGHEST = lax.Precision.HIGHEST
F32, BF16 = jnp.float32, jnp.bfloat16


def dot(a, b, over=(1, 0), precision=None):
    dims = (((over[0],), (over[1],)), ((), ()))
    return lax.dot_general(a, b, dims, precision=precision, preferred_element_type=F32)


def exact(a, b, over=(1, 0)):
    return dot(a, b, over, HIGHEST)


def same_half(rows, lanes=LANES):
    r = lax.broadcasted_iota(jnp.int32, (rows, lanes), 0)
    l = lax.broadcasted_iota(jnp.int32, (rows, lanes), 1)
    return (r < WIDTH) == (l < WIDTH)


def swap(v):
    return pltpu.roll(v, WIDTH, 1)


def columns(p):
    return slice(p * LANES, (p + 1) * LANES)


def one_head(v, den, maps):
    tokens = v[:, :WIDTH] / den
    back = swap(v)[:, :WIDTH]
    q, k, w = (exact(tokens, maps[i]) for i in range(3))
    squash = jnp.tanh(exact(q, k, (1, 1)) / math.sqrt(WIDTH) / score_cap)
    e = jnp.exp(score_cap * squash)
    attention = e / jnp.sum(e, axis=1, keepdims=True)
    out = tokens + exact(attention, w)
    d_attention = exact(back, w, (1, 1))
    d_w = exact(attention, back, (0, 0))
    d_capped = attention * (
        d_attention - jnp.sum(d_attention * attention, axis=1, keepdims=True)
    )
    d_scores = d_capped * (1.0 - squash * squash) / math.sqrt(WIDTH)
    d_q = exact(d_scores, k)
    d_k = exact(d_scores, q, (0, 0))
    grad = back + exact(d_q, maps[0], (1, 1)) + exact(d_k, maps[1], (1, 1))
    grad = grad + exact(d_w, maps[2], (1, 1))
    grad_maps = [exact(tokens, d, (0, 0)) for d in (d_q, d_k, d_w)]
    grad_mass = -jnp.sum(grad * tokens, axis=1, keepdims=True) / den
    return out, grad / den, grad_mass, grad_maps


def placed(v, half):
    r = lax.broadcasted_iota(jnp.int32, (WIDTH, LANES), 0)
    l = lax.broadcasted_iota(jnp.int32, (WIDTH, LANES), 1)
    return exact(v, (l == r + half * WIDTH).astype(F32))


def kernel(
    x_ref, we_ref, ws_ref, wa_ref, sharp_ref, maps_ref, cot_ref,
    points_out, proj_out, slice_out, maps_out,
    feature, middle, weight, squash_ref, weight_b, part, mass, xt, table, gcat,
    rc, rcm, s1, m1, rz, rzm, s2, m2, rx, rxm, s3, ry, headbuf, res,
    proj, rcp, rcw, p1, w1, pz, py, wz, a2, b2, w2, py2, pz2, wy, ab, w3, px, wx, g, gt,
    pxc, c2, pzc, c3, pyc,
    send_sem, recv_sem,
):
    at = Place()
    greeted = at.greet()
    sends = Sends(send_sem, recv_sem)
    other = 1 - at.c
    partner = at.device(c=other)
    half_mask = same_half(LANES)
    ones = half_mask.astype(F32)
    lane_low = lax.broadcasted_iota(jnp.int32, (1, LANES), 1) < WIDTH

    r = lax.broadcasted_iota(jnp.int32, (LANES, WIDTH), 0)
    l = lax.broadcasted_iota(jnp.int32, (LANES, WIDTH), 1)
    twice = ((l == r) | (l == r - WIDTH)).astype(BF16)
    wa_pair = dot(dot(twice, wa_ref[...]).astype(BF16), twice, (1, 1))
    wa_pair = jnp.where(half_mask, wa_pair, 0.0).astype(BF16)

    def sharp(p):
        return jnp.where(lane_low, sharp_ref[2 * p], sharp_ref[2 * p + 1])

    feature[...] = dot(x_ref[...], we_ref[...]).astype(BF16)
    middle[...] = dot(x_ref[...], ws_ref[...]).astype(BF16)
    mass[...] = jnp.zeros_like(mass)
    for p in range(PAIRS):
        cols = columns(p)
        raw = dot(middle[:, cols], wa_pair)
        squash = jnp.tanh(raw / (partition_affinity_bound * sharp(p)))
        e = jnp.exp(partition_affinity_bound * squash)
        w = e / exact(e, ones)
        wb = w.astype(BF16)
        squash_ref[:, cols] = squash
        weight[:, cols] = w
        weight_b[:, cols] = wb
        mass[p : p + 1, :] = jnp.sum(w, axis=0, keepdims=True)
        tok = dot(wb, feature[:, cols], (0, 0))
        back = dot(wb, cot_ref[:, cols], (0, 0))
        both = jnp.where(half_mask, tok, swap(back))
        part[p // 2, 2 * (p % 2) : 2 * (p % 2) + 2] = both.reshape(2, NZ, 8, LANES)

    greeted()
    copies = [
        sends.start(part.at[other], rc, partner),
        sends.start(mass, rcm, partner),
    ]
    xt[...] = x_ref[...].T
    sends.recv(copies)
    s1[...] = part[at.c] + rc[...]
    m1[...] = mass[...] + rcm[...]

    copies = []
    for k, there, device in at.along("x"):
        copies.append(sends.start(s1.at[there], rx.at[k - 1], device))
        copies.append(sends.start(m1, rxm.at[at.x], device))
    rxm[at.x] = m1[...]
    sends.recv(copies)
    s2[...] = s1[at.x] + jnp.sum(rx[...], axis=0)
    m2[...] = jnp.sum(rxm[...], axis=0)

    copies = []
    for k, there, device in at.along("z"):
        copies.append(sends.start(s2.at[there], rz.at[k - 1], device))
        copies.append(sends.start(m2, rzm.at[at.z], device))
    rzm[at.z] = m2[...]
    sends.recv(copies)
    s3[0] = s2[at.z] + jnp.sum(rz[...], axis=0)
    s3[1] = jnp.sum(rzm[...], axis=0)

    copies = []
    for k, there, device in at.along("y"):
        copies.append(sends.start(s3, ry.at[at.y], device))
    ry[at.y] = s3[...]
    sends.recv(copies)
    done = jnp.sum(ry[...], axis=0)

    headbuf[at.z] = done[0]
    mine = headbuf.at[at.z]
    sends.recv([sends.start(mine, mine, d) for _, _, d in at.along("z")])

    odd = lax.rem(at.x, 2)
    pair = at.c * 2 + lax.div(at.x, 2)
    rows8 = lax.broadcasted_iota(jnp.int32, (8, LANES), 0)
    mass_row = jnp.sum(jnp.where(rows8 == pair, done[1], 0.0), axis=0, keepdims=True)
    r = lax.broadcasted_iota(jnp.int32, (WIDTH, LANES), 0)
    l = lax.broadcasted_iota(jnp.int32, (WIDTH, LANES), 1)
    den = jnp.sum(jnp.where(l == r + odd * WIDTH, mass_row, 0.0), axis=1, keepdims=True)
    v = headbuf[...].reshape(WIDTH, LANES)
    v = jnp.where(odd == 1, swap(v), v)
    out, grad_sum, grad_mass, grad_maps = one_head(v, den + epsilon, maps_ref)
    both = placed(grad_sum, 0) + placed(out, 1)
    both = jnp.where(odd == 1, swap(both), both)
    res[at.c, at.x, pl.ds(0, NZ)] = both.reshape(NZ, 8, LANES)
    mass_row = jnp.sum(
        jnp.where((l == r) | (l == r + WIDTH), grad_mass, 0.0), axis=0, keepdims=True
    )
    res[at.c, at.x, NZ] = jnp.broadcast_to(mass_row, (8, LANES))

    mine = res.at[at.c, at.x]
    copies = [(k, sends.start(mine, mine, d)) for k, _, d in at.along("x")]
    passed = [sends.start(mine, mine, partner)]
    scale = 1.0 / (NY * NZ)
    table_low = placed(grad_maps[0] * scale, 1)
    table_high = placed(grad_maps[1] * scale, 0) + placed(grad_maps[2] * scale, 1)
    for k, copy in copies:
        copy.wait_recv()
        came = res.at[at.c, lax.rem(at.x + NX - k, NX)]
        passed.append(sends.start(came, came, partner))
    sends.recv(passed)

    slice_acc = jnp.zeros((LANES, LANES), F32)
    for p in range(PAIRS):
        cols = columns(p)
        c, x0 = p // 2, (p % 2) * 2
        v = res[c, x0 : x0 + 2, 0:NZ].reshape(LANES, LANES)
        gm = jnp.where(lane_low, res[c, x0, NZ, 0:1], res[c, x0 + 1, NZ, 0:1])
        gs = jnp.where(half_mask, v, 0.0).astype(BF16)
        ob = jnp.where(half_mask, swap(v), 0.0).astype(BF16)
        gw = dot(cot_ref[:, cols], ob, (1, 1)) + dot(feature[:, cols], gs, (1, 1)) + gm
        w = weight[:, cols]
        squash = squash_ref[:, cols]
        pre = w * (gw - exact(w * gw, ones))
        gr = (pre * (1.0 - squash * squash) / sharp(p)).astype(BF16)
        gcat[p] = dot(weight_b[:, cols], gs).astype(BF16)
        gcat[PAIRS + p] = dot(gr, wa_pair, (1, 1)).astype(BF16)
        slice_acc = slice_acc + dot(middle[:, cols], gr, (0, 0))

    core_copies = []
    order = [k for k, _, _ in at.along("z")] + [0]
    for k in order:
        blk = lax.rem(at.z + k, NZ)
        r = dot(xt[...], gcat[blk]).reshape(NX, NY // 2, 2, 2, 8, LANES)
        for c in range(2):
            for side in range(2):
                proj[c, blk, side] = r[:, :, side, c]
        core_copies.append(sends.start(proj.at[other, blk], rcp.at[blk], partner))
    sl = slice_acc[:WIDTH] + swap(slice_acc[WIDTH:])
    sl = jnp.where(lane_low, sl, 0.0)
    table[:, 0] = (sl + table_low).reshape(NZ, 8, LANES)
    table[:, 1] = table_high.reshape(NZ, 8, LANES)
    table_copy = sends.start(table, rcw, partner)

    half = NX // 2
    y_odd = lax.rem(at.y, 2) == 1
    y_even = lax.rem(at.y, 2) == 0
    yh = lax.div(at.y, 2)
    owed = []

    def to_side(side, src, dst):
        planned = [(j, sends.plan(src(j, yt), dst(j), yd)) for j, yt, yd in at.along("y")]
        for mine, cond in ((1, y_odd), (0, y_even)):
            group = [copy for j, copy in planned if (j + mine) % 2 == side]
            owed.append((cond, group))

            @pl.when(cond)
            def _():
                for copy in group:
                    copy.start()

        return [copy for _, copy in planned]

    c_copies, b_copies = [], []
    z_of = {k: d for k, _, d in at.along("z")}
    copies = []
    for k, copy in zip(order, core_copies):
        blk = lax.rem(at.z + k, NZ)
        copy.wait_recv()
        p1[blk] = proj[at.c, blk] + rcp[blk]
        for j, xt_, xd in at.along("x"):
            c_copies.append(sends.start(p1.at[blk, 0, xt_], pxc.at[j - 1, blk], xd))
        if k:
            copies.append(sends.start(p1.at[blk, 1, pl.ds(0, half)], pz.at[k - 1], z_of[k]))
        b_copies += to_side(
            1,
            lambda j, yt: p1.at[blk, 1, pl.ds(half, half), lax.div(yt, 2)],
            lambda j: py.at[j - 1, blk],
        )
    table_copy.wait_recv()
    w1[...] = table[...] + rcw[...]
    for k, zt, zd in at.along("z"):
        copies.append(sends.start(w1.at[zt], wz.at[k - 1], zd))

    points = jnp.zeros(points_out.shape, F32)
    for p in range(PAIRS):
        cols = columns(p)
        points = points + dot(gcat[p], we_ref[:, cols], (1, 1))
    for p in range(PAIRS):
        cols = columns(p)
        points = points + dot(gcat[PAIRS + p], ws_ref[:, cols], (1, 1))
    points_out[...] = points.astype(BF16)

    sends.recv(c_copies)
    c2[...] = p1[:, 0, at.x] + jnp.sum(pxc[...], axis=0)
    c_copies = [sends.start(c2.at[zt], pzc.at[k - 1], zd) for k, zt, zd in at.along("z")]

    sends.recv(copies)
    a2[...] = p1[at.z, 1, pl.ds(0, half)] + jnp.sum(pz[...], axis=0)
    a_copies = to_side(1, lambda j, yt: a2.at[:, lax.div(yt, 2)], lambda j: py2.at[j - 1])
    w2[...] = w1[at.z] + jnp.sum(wz[...], axis=0)
    copies = [sends.start(w2, wy.at[at.y], yd) for _, _, yd in at.along("y")]
    wy[at.y] = w2[...]
    b_next = [sends.plan(b2.at[zt], pz2.at[k - 1], zd) for k, zt, zd in at.along("z")]

    @pl.when(y_odd)
    def _():
        sends.recv(b_copies)
        b2[...] = p1[:, 1, pl.ds(half, half), yh] + jnp.sum(py[...], axis=0)
        for copy in b_next:
            copy.start()

    owed.append((y_odd, b_next))

    sends.recv(c_copies)
    c3[...] = c2[at.z] + jnp.sum(pzc[...], axis=0)
    c_copies = to_side(0, lambda j, yt: c3.at[lax.div(yt, 2)], lambda j: pyc.at[j - 1])

    sends.recv(copies)
    w3[...] = jnp.sum(wy[...], axis=0)
    copies = [sends.start(w3, wx.at[at.x], xd) for _, _, xd in at.along("x")]
    wx[at.x] = w3[...]
    ab_next = [sends.plan(ab.at[there], px.at[k - 1], xd) for k, there, xd in at.along("x")]
    owed.append((y_odd, ab_next))

    @pl.when(y_odd)
    def _():
        sends.recv(a_copies)
        sends.recv(b_next)
        ab[pl.ds(0, half)] = a2[:, yh] + jnp.sum(py2[...], axis=0)
        ab[pl.ds(half, half)] = b2[at.z] + jnp.sum(pz2[...], axis=0)
        for copy in ab_next:
            copy.start()
        sends.recv(ab_next)
        g[at.c, at.z] = ab[at.x] + jnp.sum(px[...], axis=0)

    @pl.when(y_even)
    def _():
        sends.recv(c_copies)
        g[at.c, at.z] = c3[yh] + jnp.sum(pyc[...], axis=0)

    sends.recv(copies)
    gt[at.z] = jnp.sum(wx[...], axis=0)

    mine, also = g.at[at.c, at.z], gt.at[at.z]
    copies = []
    for _, _, d in at.along("z"):
        copies.append(sends.start(mine, mine, d))
        copies.append(sends.start(also, also, d))
    sends.recv(copies)
    mine = g.at[at.c]
    copies = [sends.start(mine, mine, partner)]
    low = gt[:, 0].reshape(WIDTH, LANES)
    high = gt[:, 1].reshape(WIDTH, LANES)
    slice_out[...] = low[:, :WIDTH]
    maps_out[0] = swap(low)[:, :WIDTH]
    maps_out[1] = high[:, :WIDTH]
    maps_out[2] = swap(high)[:, :WIDTH]
    sends.recv(copies)
    for c in range(2):
        for z in range(NZ):
            proj_out[c * 8 : (c + 1) * 8, columns(z)] = g[c, z]
    sends.finish()
    for cond, group in owed:

        @pl.when(cond)
        def _():
            for copy in group:
                copy.wait_send()


def store_kernel(*refs):
    sem = refs[8]
    copies = [pltpu.make_async_copy(refs[i], refs[4 + i], sem.at[i]) for i in range(4)]
    for copy in copies:
        copy.start()
    for copy in copies:
        copy.wait()


def body(
    vertex_inputs,
    partition_embed_matrix,
    selector_embed_matrix,
    partition_affinity_matrix,
    sharpness_divisor,
    latent_query_key_value_maps,
    result_cotangent,
):
    rows, width = vertex_inputs.shape
    tile = (8, LANES)
    half, yside = NX // 2, NY // 2
    copies = 2 + 2 * 3 + 2 * 7 + 7 + 7 + 3 + 4 + 8 + 1 + 8 * 3 + 7 + 8 * 7 + 7
    copies += 4 * 7 + 3 + 3 + 7 + 2 * 7 + 1
    vmem = pl.BlockSpec(memory_space=pltpu.VMEM)
    smem = pl.BlockSpec(memory_space=pltpu.SMEM)

    def f32(*shape):
        return pltpu.VMEM(shape + tile, F32)

    results = pl.pallas_call(
        kernel,
        out_shape=(
            jax.ShapeDtypeStruct((rows, width), BF16),
            jax.ShapeDtypeStruct((16, 1024), F32),
            jax.ShapeDtypeStruct((WIDTH, WIDTH), F32),
            jax.ShapeDtypeStruct((3, WIDTH, WIDTH), F32),
        ),
        in_specs=[vmem, vmem, vmem, vmem, smem, vmem, vmem],
        out_specs=(vmem, vmem, vmem, vmem),
        scratch_shapes=[
            pltpu.VMEM((rows, width), BF16),
            pltpu.VMEM((rows, width), BF16),
            pltpu.VMEM((rows, width), F32),
            pltpu.VMEM((rows, width), F32),
            pltpu.VMEM((rows, width), BF16),
            f32(2, NX, NZ),
            f32(),
            pltpu.VMEM((width, rows), BF16),
            f32(NZ, 2),
            pltpu.VMEM((NZ, rows, LANES), BF16),
            f32(NX, NZ),
            f32(),
            f32(NX, NZ),
            f32(),
            f32(NZ - 1),
            f32(NZ),
            f32(NZ),
            f32(),
            f32(NX - 1, NZ),
            f32(NX),
            f32(2),
            f32(NY, 2),
            f32(NZ),
            f32(2, NX, NZ + 1),
            f32(2, NZ, 2, NX, yside),
            f32(NZ, 2, NX, yside),
            f32(NZ, 2),
            f32(NZ, 2, NX, yside),
            f32(NZ, 2),
            f32(NZ - 1, half, yside),
            f32(NY - 1, NZ, half),
            f32(NZ - 1, 2),
            f32(half, yside),
            f32(NZ, half),
            f32(2),
            f32(NY - 1, half),
            f32(NZ - 1, half),
            f32(NY, 2),
            f32(NX),
            f32(2),
            f32(NX - 1),
            f32(NX, 2),
            f32(2, NZ),
            f32(NZ, 2),
            f32(NX - 1, NZ, yside),
            f32(NZ, yside),
            f32(NZ - 1, yside),
            f32(yside),
            f32(NY - 1),
            pltpu.SemaphoreType.DMA((copies,)),
            pltpu.SemaphoreType.DMA((copies,)),
        ],
        compiler_params=pltpu.CompilerParams(collective_id=1, has_side_effects=True),
        name="layer",
    )(
        vertex_inputs,
        partition_embed_matrix,
        selector_embed_matrix,
        partition_affinity_matrix,
        sharpness_divisor,
        latent_query_key_value_maps,
        result_cotangent,
    )
    return pl.pallas_call(
        store_kernel,
        out_shape=tuple(jax.ShapeDtypeStruct(r.shape, r.dtype) for r in results),
        in_specs=[vmem] * 4,
        out_specs=(pl.BlockSpec(memory_space=pl.ANY),) * 4,
        scratch_shapes=[pltpu.SemaphoreType.DMA((4,))],
        name="store",
    )(*results)


def solution(mesh):
    return jax.shard_map(
        body,
        mesh=mesh,
        in_specs=(
            P(("region", "band"), None),
            P(),
            P(),
            P(),
            P(),
            P(),
            P(("region", "band"), None),
        ),
        out_specs=(P(("region", "band"), None), P("region", None), P(), P()),
        check_vma=False,
    )
```

```python
import math

import jax
import jax.numpy as jnp
from jax import lax
from jax.experimental import pallas as pl
from jax.experimental.pallas import tpu as pltpu
from jax.sharding import PartitionSpec as P

partition_affinity_bound = 8.0
score_cap = 10.0
epsilon = 1e-05

NX, NY, NZ = 4, 8, 8
MESH = pl.DeviceIdType.MESH


class Place:
    def __init__(self):
        region, band = lax.axis_index("region"), lax.axis_index("band")
        self.x, self.y = lax.div(region, NY), lax.rem(region, NY)
        self.z, self.c = lax.div(band, 2), lax.rem(band, 2)

    def device(self, x=None, y=None, z=None, c=None):
        x = self.x if x is None else x
        y = self.y if y is None else y
        z = self.z if z is None else z
        c = self.c if c is None else c
        return {"region": x * NY + y, "band": z * 2 + c}

    def along(self, axis):
        size = {"x": NX, "y": NY, "z": NZ}[axis]
        here = getattr(self, axis)
        order = sorted(range(1, size), key=lambda k: -min(k, size - k))
        for k in order:
            there = lax.rem(here + k, size)
            yield k, there, self.device(**{axis: there})

    def greet(self):
        barrier = pltpu.get_barrier_semaphore()
        count = 0
        partners = [self.device(c=1 - self.c)]
        for axis in "xyz":
            partners += [d for _, _, d in self.along(axis)]
        for d in partners:
            pl.semaphore_signal(barrier, inc=1, device_id=d, device_id_type=MESH)
            count += 1
        return lambda: pl.semaphore_wait(barrier, count)


class Sends:
    def __init__(self, send_sem, recv_sem):
        self.send_sem, self.recv_sem, self.used, self.open = send_sem, recv_sem, 0, []

    def plan(self, src, dst, device):
        i = self.used
        self.used += 1
        return pltpu.make_async_remote_copy(
            src_ref=src,
            dst_ref=dst,
            send_sem=self.send_sem.at[i],
            recv_sem=self.recv_sem.at[i],
            device_id=device,
            device_id_type=MESH,
        )

    def start(self, src, dst, device):
        copy = self.plan(src, dst, device)
        copy.start()
        self.open.append(copy)
        return copy

    def recv(self, copies):
        for copy in copies:
            copy.wait_recv()

    def finish(self):
        for copy in self.open:
            copy.wait_send()


HEADS, PAIRS, WIDTH = 8, 4, 64
LANES = 128
HIGHEST = lax.Precision.HIGHEST
F32, BF16 = jnp.float32, jnp.bfloat16


def dot(a, b, over=(1, 0), precision=None):
    dims = (((over[0],), (over[1],)), ((), ()))
    return lax.dot_general(a, b, dims, precision=precision, preferred_element_type=F32)


def exact(a, b, over=(1, 0)):
    return dot(a, b, over, HIGHEST)


def same_half(rows, lanes=LANES):
    r = lax.broadcasted_iota(jnp.int32, (rows, lanes), 0)
    l = lax.broadcasted_iota(jnp.int32, (rows, lanes), 1)
    return (r < WIDTH) == (l < WIDTH)


def swap(v):
    return pltpu.roll(v, WIDTH, 1)


def columns(p):
    return slice(p * LANES, (p + 1) * LANES)


def one_head(v, den, maps):
    tokens = v[:, :WIDTH] / den
    back = swap(v)[:, :WIDTH]
    q, k, w = (exact(tokens, maps[i]) for i in range(3))
    squash = jnp.tanh(exact(q, k, (1, 1)) / math.sqrt(WIDTH) / score_cap)
    e = jnp.exp(score_cap * squash)
    attention = e / jnp.sum(e, axis=1, keepdims=True)
    out = tokens + exact(attention, w)
    d_attention = exact(back, w, (1, 1))
    d_w = exact(attention, back, (0, 0))
    d_capped = attention * (
        d_attention - jnp.sum(d_attention * attention, axis=1, keepdims=True)
    )
    d_scores = d_capped * (1.0 - squash * squash) / math.sqrt(WIDTH)
    d_q = exact(d_scores, k)
    d_k = exact(d_scores, q, (0, 0))
    grad = back + exact(d_q, maps[0], (1, 1)) + exact(d_k, maps[1], (1, 1))
    grad = grad + exact(d_w, maps[2], (1, 1))
    grad_maps = [exact(tokens, d, (0, 0)) for d in (d_q, d_k, d_w)]
    grad_mass = -jnp.sum(grad * tokens, axis=1, keepdims=True) / den
    return out, grad / den, grad_mass, grad_maps


def placed(v, half):
    r = lax.broadcasted_iota(jnp.int32, (WIDTH, LANES), 0)
    l = lax.broadcasted_iota(jnp.int32, (WIDTH, LANES), 1)
    return exact(v, (l == r + half * WIDTH).astype(F32))


def kernel(
    x_ref, we_ref, ws_ref, wa_ref, sharp_ref, maps_ref, cot_ref,
    points_out, proj_out, slice_out, maps_out,
    feature, middle, weight, squash_ref, weight_b, part, mass, xt, table, gcat,
    rc, rcm, s1, m1, rz, rzm, s2, m2, rx, rxm, s3, ry, headbuf, res,
    proj, rcp, rcw, p1, w1, pz, py, wz, a2, b2, w2, py2, pz2, wy, ab, w3, px, wx, g, gt,
    pxc, c2, pzc, c3, pyc,
    send_sem, recv_sem,
):
    at = Place()
    greeted = at.greet()
    sends = Sends(send_sem, recv_sem)
    other = 1 - at.c
    partner = at.device(c=other)
    half_mask = same_half(LANES)
    ones = half_mask.astype(F32)
    lane_low = lax.broadcasted_iota(jnp.int32, (1, LANES), 1) < WIDTH

    r = lax.broadcasted_iota(jnp.int32, (LANES, WIDTH), 0)
    l = lax.broadcasted_iota(jnp.int32, (LANES, WIDTH), 1)
    twice = ((l == r) | (l == r - WIDTH)).astype(BF16)
    wa_pair = dot(dot(twice, wa_ref[...]).astype(BF16), twice, (1, 1))
    wa_pair = jnp.where(half_mask, wa_pair, 0.0).astype(BF16)

    def sharp(p):
        return jnp.where(lane_low, sharp_ref[2 * p], sharp_ref[2 * p + 1])

    feature[...] = dot(x_ref[...], we_ref[...]).astype(BF16)
    middle[...] = dot(x_ref[...], ws_ref[...]).astype(BF16)
    mass[...] = jnp.zeros_like(mass)
    for i in range(PAIRS):
        core = other if i < 2 else at.c
        p = core * 2 + i % 2
        cols = pl.ds(pl.multiple_of(p * LANES, LANES), LANES)
        raw = dot(middle[:, cols], wa_pair)
        squash = jnp.tanh(raw / (partition_affinity_bound * sharp(p)))
        e = jnp.exp(partition_affinity_bound * squash)
        w = e / exact(e, ones)
        wb = w.astype(BF16)
        squash_ref[:, cols] = squash
        weight[:, cols] = w
        weight_b[:, cols] = wb
        mass[i // 2, i % 2 : i % 2 + 1, :] = jnp.sum(w, axis=0, keepdims=True)
        tok = dot(wb, feature[:, cols], (0, 0))
        back = dot(wb, cot_ref[:, cols], (0, 0))
        both = jnp.where(half_mask, tok, swap(back))
        part[core, 2 * (i % 2) : 2 * (i % 2) + 2] = both.reshape(2, NZ, 8, LANES)
        if i == 1:
            greeted()
            copies = [
                sends.start(part.at[other], rc, partner),
                sends.start(mass.at[0], rcm, partner),
            ]
    xt[...] = x_ref[...].T
    sends.recv(copies)
    s1[...] = part[at.c] + rc[...]
    m1[...] = mass[1] + rcm[...]

    copies = []
    for k, there, device in at.along("x"):
        copies.append(sends.start(s1.at[there], rx.at[k - 1], device))
        copies.append(sends.start(m1, rxm.at[at.x], device))
    rxm[at.x] = m1[...]
    sends.recv(copies)
    s2[...] = s1[at.x] + jnp.sum(rx[...], axis=0)
    m2[...] = jnp.sum(rxm[...], axis=0)

    copies = []
    for k, there, device in at.along("z"):
        copies.append(sends.start(s2.at[there], rz.at[k - 1], device))
        copies.append(sends.start(m2, rzm.at[at.z], device))
    rzm[at.z] = m2[...]
    sends.recv(copies)
    s3[0] = s2[at.z] + jnp.sum(rz[...], axis=0)
    s3[1] = jnp.sum(rzm[...], axis=0)

    copies = []
    for k, there, device in at.along("y"):
        copies.append(sends.start(s3, ry.at[at.y], device))
    ry[at.y] = s3[...]
    sends.recv(copies)
    done = jnp.sum(ry[...], axis=0)

    headbuf[at.z] = done[0]
    mine = headbuf.at[at.z]
    sends.recv([sends.start(mine, mine, d) for _, _, d in at.along("z")])

    odd = lax.rem(at.x, 2)
    pair = lax.div(at.x, 2)
    rows8 = lax.broadcasted_iota(jnp.int32, (8, LANES), 0)
    mass_row = jnp.sum(jnp.where(rows8 == pair, done[1], 0.0), axis=0, keepdims=True)
    r = lax.broadcasted_iota(jnp.int32, (WIDTH, LANES), 0)
    l = lax.broadcasted_iota(jnp.int32, (WIDTH, LANES), 1)
    den = jnp.sum(jnp.where(l == r + odd * WIDTH, mass_row, 0.0), axis=1, keepdims=True)
    v = headbuf[...].reshape(WIDTH, LANES)
    v = jnp.where(odd == 1, swap(v), v)
    out, grad_sum, grad_mass, grad_maps = one_head(v, den + epsilon, maps_ref)
    both = placed(grad_sum, 0) + placed(out, 1)
    both = jnp.where(odd == 1, swap(both), both)
    res[at.c, at.x, pl.ds(0, NZ)] = both.reshape(NZ, 8, LANES)
    mass_row = jnp.sum(
        jnp.where((l == r) | (l == r + WIDTH), grad_mass, 0.0), axis=0, keepdims=True
    )
    res[at.c, at.x, NZ] = jnp.broadcast_to(mass_row, (8, LANES))

    mine = res.at[at.c, at.x]
    copies = [(k, sends.start(mine, mine, d)) for k, _, d in at.along("x")]
    passed = [sends.start(mine, mine, partner)]
    scale = 1.0 / (NY * NZ)
    table_low = placed(grad_maps[0] * scale, 1)
    table_high = placed(grad_maps[1] * scale, 0) + placed(grad_maps[2] * scale, 1)
    for k, copy in copies:
        copy.wait_recv()
        came = res.at[at.c, lax.rem(at.x + NX - k, NX)]
        passed.append(sends.start(came, came, partner))
    sends.recv(passed)

    slice_acc = jnp.zeros((LANES, LANES), F32)
    for p in range(PAIRS):
        cols = columns(p)
        c, x0 = p // 2, (p % 2) * 2
        v = res[c, x0 : x0 + 2, 0:NZ].reshape(LANES, LANES)
        gm = jnp.where(lane_low, res[c, x0, NZ, 0:1], res[c, x0 + 1, NZ, 0:1])
        gs = jnp.where(half_mask, v, 0.0).astype(BF16)
        ob = jnp.where(half_mask, swap(v), 0.0).astype(BF16)
        gw = dot(cot_ref[:, cols], ob, (1, 1)) + dot(feature[:, cols], gs, (1, 1)) + gm
        w = weight[:, cols]
        squash = squash_ref[:, cols]
        pre = w * (gw - exact(w * gw, ones))
        gr = (pre * (1.0 - squash * squash) / sharp(p)).astype(BF16)
        gcat[p] = dot(weight_b[:, cols], gs).astype(BF16)
        gcat[PAIRS + p] = dot(gr, wa_pair, (1, 1)).astype(BF16)
        slice_acc = slice_acc + dot(middle[:, cols], gr, (0, 0))

    core_copies = []
    order = [k for k, _, _ in at.along("z")] + [0]
    for k in order:
        blk = lax.rem(at.z + k, NZ)
        r = dot(xt[...], gcat[blk]).reshape(NX, NY // 2, 2, 2, 8, LANES)
        for c in range(2):
            for side in range(2):
                proj[c, blk, side] = r[:, :, side, c]
        core_copies.append(sends.start(proj.at[other, blk], rcp.at[blk], partner))
    sl = slice_acc[:WIDTH] + swap(slice_acc[WIDTH:])
    sl = jnp.where(lane_low, sl, 0.0)
    table[:, 0] = (sl + table_low).reshape(NZ, 8, LANES)
    table[:, 1] = table_high.reshape(NZ, 8, LANES)
    table_copy = sends.start(table, rcw, partner)

    half = NX // 2
    y_odd = lax.rem(at.y, 2) == 1
    y_even = lax.rem(at.y, 2) == 0
    yh = lax.div(at.y, 2)
    owed = []

    def to_side(side, src, dst):
        planned = [(j, sends.plan(src(j, yt), dst(j), yd)) for j, yt, yd in at.along("y")]
        for mine, cond in ((1, y_odd), (0, y_even)):
            group = [copy for j, copy in planned if (j + mine) % 2 == side]
            owed.append((cond, group))

            @pl.when(cond)
            def _():
                for copy in group:
                    copy.start()

        return [copy for _, copy in planned]

    c_copies, b_copies = [], []
    z_of = {k: d for k, _, d in at.along("z")}
    copies = []
    for k, copy in zip(order, core_copies):
        blk = lax.rem(at.z + k, NZ)
        copy.wait_recv()
        p1[blk] = proj[at.c, blk] + rcp[blk]
        for j, xt_, xd in at.along("x"):
            c_copies.append(sends.start(p1.at[blk, 0, xt_], pxc.at[j - 1, blk], xd))
        if k:
            copies.append(sends.start(p1.at[blk, 1, pl.ds(0, half)], pz.at[k - 1], z_of[k]))
        b_copies += to_side(
            1,
            lambda j, yt: p1.at[blk, 1, pl.ds(half, half), lax.div(yt, 2)],
            lambda j: py.at[j - 1, blk],
        )
    table_copy.wait_recv()
    w1[...] = table[...] + rcw[...]
    for k, zt, zd in at.along("z"):
        copies.append(sends.start(w1.at[zt], wz.at[k - 1], zd))

    points = jnp.zeros(points_out.shape, F32)
    for p in range(PAIRS):
        cols = columns(p)
        points = points + dot(gcat[p], we_ref[:, cols], (1, 1))
    for p in range(PAIRS):
        cols = columns(p)
        points = points + dot(gcat[PAIRS + p], ws_ref[:, cols], (1, 1))
    points_out[...] = points.astype(BF16)

    sends.recv(c_copies)
    c2[...] = p1[:, 0, at.x] + jnp.sum(pxc[...], axis=0)
    c_copies = [sends.start(c2.at[zt], pzc.at[k - 1], zd) for k, zt, zd in at.along("z")]

    sends.recv(copies)
    a2[...] = p1[at.z, 1, pl.ds(0, half)] + jnp.sum(pz[...], axis=0)
    a_copies = to_side(1, lambda j, yt: a2.at[:, lax.div(yt, 2)], lambda j: py2.at[j - 1])
    w2[...] = w1[at.z] + jnp.sum(wz[...], axis=0)
    copies = [sends.start(w2, wy.at[at.y], yd) for _, _, yd in at.along("y")]
    wy[at.y] = w2[...]
    b_next = [sends.plan(b2.at[zt], pz2.at[k - 1], zd) for k, zt, zd in at.along("z")]

    @pl.when(y_odd)
    def _():
        sends.recv(b_copies)
        b2[...] = p1[:, 1, pl.ds(half, half), yh] + jnp.sum(py[...], axis=0)
        for copy in b_next:
            copy.start()

    owed.append((y_odd, b_next))

    sends.recv(c_copies)
    c3[...] = c2[at.z] + jnp.sum(pzc[...], axis=0)
    c_copies = to_side(0, lambda j, yt: c3.at[lax.div(yt, 2)], lambda j: pyc.at[j - 1])

    sends.recv(copies)
    w3[...] = jnp.sum(wy[...], axis=0)
    copies = [sends.start(w3, wx.at[at.x], xd) for _, _, xd in at.along("x")]
    wx[at.x] = w3[...]
    ab_next = [sends.plan(ab.at[there], px.at[k - 1], xd) for k, there, xd in at.along("x")]
    owed.append((y_odd, ab_next))

    @pl.when(y_odd)
    def _():
        sends.recv(a_copies)
        sends.recv(b_next)
        ab[pl.ds(0, half)] = a2[:, yh] + jnp.sum(py2[...], axis=0)
        ab[pl.ds(half, half)] = b2[at.z] + jnp.sum(pz2[...], axis=0)
        for copy in ab_next:
            copy.start()
        sends.recv(ab_next)
        g[at.c, at.z] = ab[at.x] + jnp.sum(px[...], axis=0)

    @pl.when(y_even)
    def _():
        sends.recv(c_copies)
        g[at.c, at.z] = c3[yh] + jnp.sum(pyc[...], axis=0)

    sends.recv(copies)
    gt[at.z] = jnp.sum(wx[...], axis=0)

    mine, also = g.at[at.c, at.z], gt.at[at.z]
    copies = []
    for _, _, d in at.along("z"):
        copies.append(sends.start(mine, mine, d))
        copies.append(sends.start(also, also, d))
    sends.recv(copies)
    mine = g.at[at.c]
    copies = [sends.start(mine, mine, partner)]
    low = gt[:, 0].reshape(WIDTH, LANES)
    high = gt[:, 1].reshape(WIDTH, LANES)
    slice_out[...] = low[:, :WIDTH]
    maps_out[0] = swap(low)[:, :WIDTH]
    maps_out[1] = high[:, :WIDTH]
    maps_out[2] = swap(high)[:, :WIDTH]
    sends.recv(copies)
    for c in range(2):
        for z in range(NZ):
            proj_out[c * 8 : (c + 1) * 8, columns(z)] = g[c, z]
    sends.finish()
    for cond, group in owed:

        @pl.when(cond)
        def _():
            for copy in group:
                copy.wait_send()


def store_kernel(*refs):
    sem = refs[8]
    copies = [pltpu.make_async_copy(refs[i], refs[4 + i], sem.at[i]) for i in range(4)]
    for copy in copies:
        copy.start()
    for copy in copies:
        copy.wait()


def body(
    vertex_inputs,
    partition_embed_matrix,
    selector_embed_matrix,
    partition_affinity_matrix,
    sharpness_divisor,
    latent_query_key_value_maps,
    result_cotangent,
):
    rows, width = vertex_inputs.shape
    tile = (8, LANES)
    half, yside = NX // 2, NY // 2
    copies = 2 + 2 * 3 + 2 * 7 + 7 + 7 + 3 + 4 + 8 + 1 + 8 * 3 + 7 + 8 * 7 + 7
    copies += 4 * 7 + 3 + 3 + 7 + 2 * 7 + 1
    vmem = pl.BlockSpec(memory_space=pltpu.VMEM)
    smem = pl.BlockSpec(memory_space=pltpu.SMEM)

    def f32(*shape):
        return pltpu.VMEM(shape + tile, F32)

    results = pl.pallas_call(
        kernel,
        out_shape=(
            jax.ShapeDtypeStruct((rows, width), BF16),
            jax.ShapeDtypeStruct((16, 1024), F32),
            jax.ShapeDtypeStruct((WIDTH, WIDTH), F32),
            jax.ShapeDtypeStruct((3, WIDTH, WIDTH), F32),
        ),
        in_specs=[vmem, vmem, vmem, vmem, smem, vmem, vmem],
        out_specs=(vmem, vmem, vmem, vmem),
        scratch_shapes=[
            pltpu.VMEM((rows, width), BF16),
            pltpu.VMEM((rows, width), BF16),
            pltpu.VMEM((rows, width), F32),
            pltpu.VMEM((rows, width), F32),
            pltpu.VMEM((rows, width), BF16),
            f32(2, NX, NZ),
            f32(2),
            pltpu.VMEM((width, rows), BF16),
            f32(NZ, 2),
            pltpu.VMEM((NZ, rows, LANES), BF16),
            f32(NX, NZ),
            f32(),
            f32(NX, NZ),
            f32(),
            f32(NZ - 1),
            f32(NZ),
            f32(NZ),
            f32(),
            f32(NX - 1, NZ),
            f32(NX),
            f32(2),
            f32(NY, 2),
            f32(NZ),
            f32(2, NX, NZ + 1),
            f32(2, NZ, 2, NX, yside),
            f32(NZ, 2, NX, yside),
            f32(NZ, 2),
            f32(NZ, 2, NX, yside),
            f32(NZ, 2),
            f32(NZ - 1, half, yside),
            f32(NY - 1, NZ, half),
            f32(NZ - 1, 2),
            f32(half, yside),
            f32(NZ, half),
            f32(2),
            f32(NY - 1, half),
            f32(NZ - 1, half),
            f32(NY, 2),
            f32(NX),
            f32(2),
            f32(NX - 1),
            f32(NX, 2),
            f32(2, NZ),
            f32(NZ, 2),
            f32(NX - 1, NZ, yside),
            f32(NZ, yside),
            f32(NZ - 1, yside),
            f32(yside),
            f32(NY - 1),
            pltpu.SemaphoreType.DMA((copies,)),
            pltpu.SemaphoreType.DMA((copies,)),
        ],
        compiler_params=pltpu.CompilerParams(collective_id=1, has_side_effects=True),
        name="layer",
    )(
        vertex_inputs,
        partition_embed_matrix,
        selector_embed_matrix,
        partition_affinity_matrix,
        sharpness_divisor,
        latent_query_key_value_maps,
        result_cotangent,
    )
    return pl.pallas_call(
        store_kernel,
        out_shape=tuple(jax.ShapeDtypeStruct(r.shape, r.dtype) for r in results),
        in_specs=[vmem] * 4,
        out_specs=(pl.BlockSpec(memory_space=pl.ANY),) * 4,
        scratch_shapes=[pltpu.SemaphoreType.DMA((4,))],
        name="store",
    )(*results)


def solution(mesh):
    return jax.shard_map(
        body,
        mesh=mesh,
        in_specs=(
            P(("region", "band"), None),
            P(),
            P(),
            P(),
            P(),
            P(),
            P(("region", "band"), None),
        ),
        out_specs=(P(("region", "band"), None), P("region", None), P(), P()),
        check_vma=False,
    )
```
